32 devices in a mesh: groups: 2 (over x), chan: 16 (over z, y, core).
Axes of the slice: x: 2, y: 2, z: 4, core: 2. Of those that a mesh axis runs over, the one named last changes fastest.
Arguments:
- samples: bfloat16 [512, 2048], P(('groups', 'chan')), parts along dimension 0, may hold values from -6 to 6
- scales: bfloat16 [512], P(('groups', 'chan')), parts along dimension 0, may hold values from 0.5 to 2
- bin_ids: int32 [16, 16], replicated, may hold values from 0 to 15, as said below
- owner_table: int32 [16], replicated, may hold values from 0 to 15, each once
Outputs:
- stacks: float32 [32, 16640], P(('groups', 'chan')), parts along dimension 0
The draws below stay inside these ranges and needn't reach their ends.
There are 2 independent parts, one for each index of `groups`. The reference program is written for one: setup_inputs(seed, part) draws one part's arguments, and reference() takes and returns one part's arrays. A program takes and returns all parts, laid end to end along the dimension named above; an argument that names none is the same for every part. Nothing has to cross between parts.
Inputs may be any that keep to these rules, and one draw needn't show every extreme that they name: `bin_ids`: each bin holds at most 32 tiles, and some bin exactly 32; every bin holds at least one. `owner_table`: each device owns exactly one bin.
All inputs are finite; a program needn't handle non-finite values.
Results may differ from the reference program's by a relative error of at most 0.0003.
Values may be sent and summed in bfloat16 or wider, within the bound.
No kernel may reach another device: no remote copies, remote signals or barrier semaphores. Data moves between devices by JAX's collectives and lax.ppermute only.
A program may use at most 64 MiB of HBM per device.

```python
import math
import jax
import jax.numpy as jnp
from jax import lax

CH_DEV = 16
REC = 2048
LAG = 32
LAGS = 65
BLOCKS = 16
CHANNELS = 256


def draw_bin_ids(key, part):
    first_key = jax.random.fold_in(key, 11)
    second_key = jax.random.fold_in(key, 12)
    ranking = jnp.arange(BLOCKS, dtype=jnp.int32)
    counts = jnp.where(ranking < BLOCKS // 4, 2 * BLOCKS, jnp.where(ranking < BLOCKS // 2, BLOCKS // 2, 3 * BLOCKS // 4)).astype(jnp.int32)
    bounds = jnp.cumsum(counts)
    places_all = jnp.arange(BLOCKS * BLOCKS, dtype=jnp.int32)
    rank_of = jnp.sum((places_all[:, None] >= bounds[None, :]).astype(jnp.int32), axis=1)
    shuffle = jax.random.permutation(first_key, BLOCKS).astype(jnp.int32)
    labels = shuffle[rank_of]
    places = jax.random.permutation(second_key, BLOCKS * BLOCKS)
    flat_bins = jnp.zeros((BLOCKS * BLOCKS,), jnp.int32).at[places].set(labels)
    return flat_bins.reshape(BLOCKS, BLOCKS).astype(jnp.int32)


def block_scale(rng, shape, split, smallest, high):
    level = 1.0
    for dim, blocks in split:
        steps = jax.random.uniform(jax.random.fold_in(jax.random.fold_in(rng, 6), dim), (blocks,), jnp.float32, smallest / len(split), high / len(split))
        level = level * jnp.repeat(jnp.exp(steps), shape[dim] // blocks).reshape((-1,) + (1,) * (len(shape) - 1 - dim))
    return level


def noise(rng, extent, deviation, limit, cuts=(), kind=jnp.bfloat16):
    gain = block_scale(rng, extent, cuts, -0.22, 0.18) if cuts else 1.0
    values = jax.random.normal(rng, extent, jnp.float32) * deviation * gain
    return jnp.minimum(jnp.maximum(values, -limit), limit).astype(kind)


def setup_inputs(seed: int = 0, part: int = 0) -> dict:
    key_of = jax.random.split(jax.random.key(seed), 5)
    own_keys = jax.random.split(jax.random.fold_in(key_of[4], part), 5)
    return {
        "samples": noise(own_keys[0], (CHANNELS, REC), 1.0, 6.0, ((0, 16),)),
        "scales": jnp.clip(jnp.exp(math.log(2.0) - 1.3862944 * jax.random.uniform(own_keys[1], (CHANNELS,), jnp.float32) ** block_scale(own_keys[1], (CHANNELS,), ((0, 16),), -0.2, 0.2)), 0.5, 2.0).astype(jnp.bfloat16),
        "bin_ids": draw_bin_ids(jax.random.fold_in(key_of[4], 71), part),
        "owner_table": jax.random.permutation(key_of[3], BLOCKS).astype(jnp.int32),
    }


def unfold(record):
    span_len = record.shape[1] - 2 * LAG
    middle = record[:, LAG:LAG + span_len]
    stacked = jnp.stack([jnp.pad(middle, ((0, 0), (offset, 2 * LAG - offset))) for offset in range(LAGS)], axis=1)
    return stacked.reshape(record.shape[0] * LAGS, record.shape[1])

def reference(samples, scales, bin_ids, owner_table):
    span_len = REC - 2 * LAG
    per_dev = CH_DEV
    all_scales = scales.astype(jnp.float32)

    def visit_row(running, block_index):
        record = lax.dynamic_slice_in_dim(samples, block_index * per_dev, per_dev, 0)
        weights = lax.dynamic_slice_in_dim(all_scales, block_index * per_dev, per_dev, 0)
        unfolded = unfold(record)
        products = jnp.dot(unfolded, samples.T, preferred_element_type=jnp.float32)
        tile_set = products.reshape(per_dev, LAGS, CHANNELS) * weights[:, None, None] * all_scales[None, None, :]
        tile_set = tile_set.reshape(per_dev, LAGS, BLOCKS, per_dev).transpose(2, 0, 1, 3)
        row_bins = lax.dynamic_index_in_dim(bin_ids, block_index, 0, keepdims=False)
        slot_ids = owner_table[row_bins]
        return (running.at[slot_ids].add(tile_set), None)
    initial = jnp.zeros((BLOCKS, per_dev, LAGS, per_dev), jnp.float32)
    result = lax.scan(visit_row, initial, jnp.arange(BLOCKS, dtype=jnp.int32))
    totals = result[0]
    counts = lax.optimization_barrier(jnp.sum((bin_ids.reshape(-1)[:, None] == jnp.arange(BLOCKS, dtype=jnp.int32)[None, :]).astype(jnp.float32), axis=0))
    slot_counts = jnp.zeros((BLOCKS,), jnp.float32).at[owner_table].set(counts)
    stacks = totals / jnp.sqrt(slot_counts * span_len)[:, None, None, None]
    return stacks.reshape(BLOCKS, per_dev * LAGS * per_dev)
```

```python
import functools

import jax
import jax.numpy as jnp
from jax import lax
from jax.experimental import pallas as pl
from jax.experimental.pallas import tpu as pltpu
from jax.sharding import PartitionSpec as P

LAG = 32
LAGS = 65
CH = 16
STEP = 16
LANES = CH * STEP
FINE = 8
COARSE = 16
ROWS = FINE * COARSE
HEAD = ROWS + 8
REACH = LAG // STEP
SHIFTS = 2 * REACH + 1
OUT_LANES = LAGS * CH

VMEM = pl.BlockSpec(memory_space=pltpu.VMEM)
SMEM = pl.BlockSpec(memory_space=pltpu.SMEM)
ANY = pl.BlockSpec(memory_space=pl.ANY)


def piece_offset(devices, index):
    far = devices // 4
    return (
        lax.rem(index, far) * 4 + lax.rem(lax.div(index, far), 2) * 2 + lax.div(index, 2 * far)
    )


def prep_kernel(samples_ref, scales_ref, piece_ref, turned_ref):
    samples = samples_ref[...].astype(jnp.float32)
    for u2 in range(COARSE):
        turned_ref[u2 * 128 : (u2 + 1) * 128, 0:CH] = samples[:, u2 * 128 : (u2 + 1) * 128].T
    for u1 in range(FINE):
        parts = [
            turned_ref[pl.ds(STEP * u1 + v, COARSE, stride=128), 0:CH] for v in range(STEP)
        ]
        piece_ref[u1 * COARSE : (u1 + 1) * COARSE, :] = jnp.concatenate(parts, axis=1).astype(
            jnp.bfloat16
        )
    scales = scales_ref[...].astype(jnp.float32)
    piece_ref[ROWS:HEAD, :] = jnp.broadcast_to(
        jnp.concatenate([scales] * STEP, axis=1), (HEAD - ROWS, LANES)
    ).astype(jnp.bfloat16)


def prep(samples, scales):
    return pl.pallas_call(
        prep_kernel,
        out_shape=jax.ShapeDtypeStruct((HEAD, LANES), jnp.bfloat16),
        in_specs=[VMEM, VMEM],
        out_specs=VMEM,
        scratch_shapes=[pltpu.VMEM((COARSE * 128, 128), jnp.float32)],
        compiler_params=pltpu.CompilerParams(vmem_limit_bytes=8 << 20),
        name="prep",
    )(samples, scales.reshape(1, CH))


def pairs_kernel(devices, own_ref, bins_ref, owner_ref, list_ref):
    own = own_ref[0]
    own_bin = jnp.int32(0)
    for i in range(devices):
        own_bin = jnp.where(owner_ref[i] == own, i, own_bin)

    def row(i, found):
        list_ref[i] = found
        p = own ^ piece_offset(devices, i)
        for j in range(devices):
            q = own ^ piece_offset(devices, jnp.int32(j))
            list_ref[devices + 1 + found] = j
            found = found + jnp.where(bins_ref[p, q] == own_bin, 1, 0)
        return found

    list_ref[devices] = lax.fori_loop(0, devices, row, jnp.int32(0))


def find_pairs(devices, own, bin_ids, owner_table):
    return pl.pallas_call(
        functools.partial(pairs_kernel, devices),
        out_shape=jax.ShapeDtypeStruct((devices + 1 + devices * devices + 1,), jnp.int32),
        in_specs=[SMEM] * 3,
        out_specs=SMEM,
        compiler_params=pltpu.CompilerParams(vmem_limit_bytes=1 << 20),
        name="pairs",
    )(own, bin_ids, owner_table)


def split(value):
    high = value.astype(jnp.bfloat16)
    return high, (value - high.astype(jnp.float32)).astype(jnp.bfloat16)


def stack_kernel(
    devices, span, list_ref, near_ref, far_ref, out_ref, x_ref, ah_ref, al_ref, at_ref, yh_ref, yl_ref, sem
):
    half = devices // 2
    depth = devices * ROWS
    slab = devices * COARSE
    copies = [
        pltpu.make_async_copy(near_ref, x_ref.at[pl.ds(0, half)], sem.at[0]),
        pltpu.make_async_copy(far_ref, x_ref.at[pl.ds(half, half)], sem.at[1]),
    ]
    for copy in copies:
        copy.start()
    row = lax.broadcasted_iota(jnp.int32, (ROWS, LANES), 0)
    fine, coarse = row // COARSE, row % COARSE
    u = FINE * coarse + fine
    inside = (u >= REACH) & (u < ROWS - REACH)
    for i in range(devices):
        if i % half == 0:
            copies[i // half].wait()
        scale = x_ref[i, ROWS : ROWS + 1, :].astype(jnp.float32)
        value = jnp.where(inside, x_ref[i, 0:ROWS, :].astype(jnp.float32) * scale, 0.0)
        high, low = split(value)
        for u1 in range(FINE):
            at = (u1 * devices + i) * COARSE
            ah_ref[at : at + COARSE, :] = high[u1 * COARSE : (u1 + 1) * COARSE]
            al_ref[at : at + COARSE, :] = low[u1 * COARSE : (u1 + 1) * COARSE]
    for k in range(0, depth, 128):
        at_ref[0:LANES, k : k + 128] = ah_ref[k : k + 128, :].T
        at_ref[LANES : 2 * LANES, k : k + 128] = al_ref[k : k + 128, :].T

    def sum_partners(i, carry):
        def add(place, total):
            j = list_ref[devices + 1 + place]
            scale = x_ref[j, ROWS : ROWS + 1, :].astype(jnp.float32)
            return total + x_ref[j, 0:ROWS, :].astype(jnp.float32) * scale

        total = lax.fori_loop(
            list_ref[i], list_ref[i + 1], add, jnp.zeros((ROWS, LANES), jnp.float32)
        )

        def put(u1, value):
            high, low = split(value)
            at = pl.multiple_of(((u1 + REACH) * devices + i) * COARSE, COARSE)
            yh_ref[pl.ds(at, COARSE), :] = high
            yl_ref[pl.ds(at, COARSE), :] = low

        for u1 in range(FINE):
            put(u1, total[u1 * COARSE : (u1 + 1) * COARSE])
        for u1 in range(REACH):
            put(u1 + FINE, pltpu.roll(total[u1 * COARSE : (u1 + 1) * COARSE], COARSE - 1, 0))
        for u1 in range(FINE - REACH, FINE):
            put(u1 - FINE, pltpu.roll(total[u1 * COARSE : (u1 + 1) * COARSE], 1, 0))
        return carry

    lax.fori_loop(0, devices, sum_partners, 0)
    products = []
    for j in range(SHIFTS):
        both = jnp.dot(
            at_ref[...], yh_ref[j * slab : j * slab + depth, :], preferred_element_type=jnp.float32
        )
        rest = jnp.dot(
            at_ref[0:LANES, :],
            yl_ref[j * slab : j * slab + depth, :],
            preferred_element_type=jnp.float32,
        )
        products.append(both[0:LANES] + both[LANES : 2 * LANES] + rest)
    product = jnp.concatenate(products, axis=1)
    stack = jnp.zeros((CH, OUT_LANES), jnp.float32)
    for v in range(STEP):
        stack = stack + product[CH * v : CH * (v + 1), CH * v : CH * v + OUT_LANES]
    count = list_ref[devices].astype(jnp.float32)
    stack = stack / jnp.sqrt(jnp.full((CH, OUT_LANES), count * span, jnp.float32))
    for a in range(CH):
        out_ref[0:1, a * OUT_LANES : (a + 1) * OUT_LANES] = stack[a : a + 1]


def stack_bin(devices, span, pairs, near, far):
    depth = devices * ROWS
    extended = devices * COARSE * (FINE + 2 * REACH)
    return pl.pallas_call(
        functools.partial(stack_kernel, devices, float(span)),
        out_shape=jax.ShapeDtypeStruct((1, CH * OUT_LANES), jnp.float32),
        in_specs=[SMEM, ANY, ANY],
        out_specs=VMEM,
        scratch_shapes=[
            pltpu.VMEM((devices, HEAD, LANES), jnp.bfloat16),
            pltpu.VMEM((depth, LANES), jnp.bfloat16),
            pltpu.VMEM((depth, LANES), jnp.bfloat16),
            pltpu.VMEM((2 * LANES, depth), jnp.bfloat16),
            pltpu.VMEM((extended, LANES), jnp.bfloat16),
            pltpu.VMEM((extended, LANES), jnp.bfloat16),
            pltpu.SemaphoreType.DMA((2,)),
        ],
        compiler_params=pltpu.CompilerParams(
            vmem_limit_bytes=(8 << 20) + devices * (5 << 18)
        ),
        name="stack",
    )(pairs, near, far)


def on_device(samples, scales, bin_ids, owner_table):
    devices = lax.axis_size("chan")
    span = samples.shape[1] - 2 * LAG
    own = lax.axis_index("chan").reshape(1).astype(jnp.int32)

    def swap(value, offset):
        return lax.ppermute(value, "chan", [(i, i ^ offset) for i in range(devices)])

    piece = prep(samples, scales)
    column = [piece] + [swap(piece, offset) for offset in range(4, devices, 4)]
    plane = column + [swap(one, 2) for one in column]
    near = jnp.stack(plane)
    far = swap(near, 1)
    pairs = find_pairs(devices, own, bin_ids, owner_table)
    return stack_bin(devices, span, pairs, near, far)


def solution(mesh):
    placed = (P(("groups", "chan"), None), P(("groups", "chan")), P(), P())
    return jax.shard_map(
        on_device,
        mesh=mesh,
        in_specs=placed,
        out_specs=P(("groups", "chan"), None),
        check_vma=False,
    )
```

```python
import functools

import jax
import jax.numpy as jnp
from jax import lax
from jax.experimental import pallas as pl
from jax.experimental.pallas import tpu as pltpu
from jax.sharding import PartitionSpec as P

LAG = 32
LAGS = 65
CH = 16
STEP = 16
LANES = CH * STEP
FINE = 8
COARSE = 16
ROWS = FINE * COARSE
HEAD = ROWS + 8
REACH = LAG // STEP
SHIFTS = 2 * REACH + 1
OUT_LANES = LAGS * CH
GROUPS = 4

VMEM = pl.BlockSpec(memory_space=pltpu.VMEM)
SMEM = pl.BlockSpec(memory_space=pltpu.SMEM)
ANY = pl.BlockSpec(memory_space=pl.ANY)
HBM = pl.BlockSpec(memory_space=pltpu.HBM)


def piece_offset(devices, index):
    far = devices // GROUPS
    return (
        lax.rem(index, far) * 4 + lax.rem(lax.div(index, far), 2) * 2 + lax.div(index, 2 * far)
    )


def prep_kernel(samples_ref, scales_ref, piece_ref, x_ref, s_ref, turned_ref, sem):
    copies = [
        pltpu.make_async_copy(samples_ref, x_ref, sem.at[0]),
        pltpu.make_async_copy(scales_ref, s_ref, sem.at[1]),
    ]
    for copy in copies:
        copy.start()
    copies[0].wait()
    samples = x_ref[...].astype(jnp.float32)
    for u2 in range(COARSE):
        turned_ref[u2 * 128 : (u2 + 1) * 128, 0:CH] = samples[:, u2 * 128 : (u2 + 1) * 128].T
    for u1 in range(FINE):
        parts = [
            turned_ref[pl.ds(STEP * u1 + v, COARSE, stride=128), 0:CH] for v in range(STEP)
        ]
        piece_ref[u1 * COARSE : (u1 + 1) * COARSE, :] = jnp.concatenate(parts, axis=1).astype(
            jnp.bfloat16
        )
    copies[1].wait()
    scales = s_ref[...].astype(jnp.float32)
    piece_ref[ROWS:HEAD, :] = jnp.broadcast_to(
        jnp.concatenate([scales] * STEP, axis=1), (HEAD - ROWS, LANES)
    ).astype(jnp.bfloat16)


def prep(samples, scales):
    return pl.pallas_call(
        prep_kernel,
        out_shape=jax.ShapeDtypeStruct((HEAD, LANES), jnp.bfloat16),
        in_specs=[HBM, HBM],
        out_specs=VMEM,
        scratch_shapes=[
            pltpu.VMEM(samples.shape, jnp.bfloat16),
            pltpu.VMEM((1, CH), jnp.bfloat16),
            pltpu.VMEM((COARSE * 128, 128), jnp.float32),
            pltpu.SemaphoreType.DMA((2,)),
        ],
        compiler_params=pltpu.CompilerParams(vmem_limit_bytes=4 << 20),
        name="prep",
    )(
        pltpu.with_memory_space_constraint(samples, pltpu.HBM),
        pltpu.with_memory_space_constraint(scales.reshape(1, CH), pltpu.HBM),
    )


def pairs_kernel(devices, own_ref, bins_ref, owner_ref, list_ref):
    own = own_ref[0]
    early_at, late_at = 2, 3 + devices * devices
    first_late = devices - devices // GROUPS
    own_bin = jnp.int32(0)
    for i in range(devices):
        own_bin = jnp.where(owner_ref[i] == own, i, own_bin)

    def row(i, found):
        early, late = found
        p = own ^ piece_offset(devices, i)
        for j in range(devices):
            q = own ^ piece_offset(devices, jnp.int32(j))
            hit = jnp.where(bins_ref[p, q] == own_bin, 1, 0)
            code = i * devices + j
            if j < first_late:
                list_ref[early_at + early] = code
                early = early + hit
            else:
                list_ref[late_at + late] = code
                late = late + hit
        return early, late

    early, late = lax.fori_loop(0, devices, row, (jnp.int32(0), jnp.int32(0)))
    list_ref[0] = early
    list_ref[1] = late


def find_pairs(devices, own, bin_ids, owner_table):
    return pl.pallas_call(
        functools.partial(pairs_kernel, devices),
        out_shape=jax.ShapeDtypeStruct((2 * devices * devices + 4,), jnp.int32),
        in_specs=[SMEM] * 3,
        out_specs=SMEM,
        compiler_params=pltpu.CompilerParams(vmem_limit_bytes=1 << 20),
        cost_estimate=pl.CostEstimate(flops=10_000_000, bytes_accessed=1 << 20, transcendentals=0),
        name="pairs",
    )(own, bin_ids, owner_table)


def split(value):
    high = value.astype(jnp.bfloat16)
    return high, (value - high.astype(jnp.float32)).astype(jnp.bfloat16)


def inside_rows():
    row = lax.broadcasted_iota(jnp.int32, (ROWS, LANES), 0)
    u = FINE * (row % COARSE) + row // COARSE
    return (u >= REACH) & (u < ROWS - REACH)


def turn_group(load, members, turned_ref, high_ref, low_ref):
    inside = inside_rows()
    for i in range(members):
        scale = load(i, ROWS, ROWS + 1)
        high, low = split(jnp.where(inside, load(i, 0, ROWS) * scale, 0.0))
        for u1 in range(FINE):
            at = (u1 * members + i) * COARSE
            high_ref[at : at + COARSE, :] = high[u1 * COARSE : (u1 + 1) * COARSE]
            low_ref[at : at + COARSE, :] = low[u1 * COARSE : (u1 + 1) * COARSE]
    for k in range(0, members * ROWS, 128):
        turned_ref[0:LANES, k : k + 128] = high_ref[k : k + 128, :].T
        turned_ref[LANES : 2 * LANES, k : k + 128] = low_ref[k : k + 128, :].T


def loader(ref):
    return lambda i, start, stop: ref[i, start:stop, :].astype(jnp.float32)


def turn_kernel(x_hbm, turned_ref, x_ref, high_ref, low_ref, sem):
    copy = pltpu.make_async_copy(x_hbm, x_ref, sem)
    copy.start()
    copy.wait()
    turn_group(loader(x_ref), x_ref.shape[0], turned_ref, high_ref, low_ref)


def turn(pieces):
    members = pieces.shape[0]
    return pl.pallas_call(
        turn_kernel,
        out_shape=jax.ShapeDtypeStruct((2 * LANES, members * ROWS), jnp.bfloat16),
        in_specs=[ANY],
        out_specs=VMEM,
        scratch_shapes=[
            pltpu.VMEM(pieces.shape, jnp.bfloat16),
            pltpu.VMEM((members * ROWS, LANES), jnp.bfloat16),
            pltpu.VMEM((members * ROWS, LANES), jnp.bfloat16),
            pltpu.SemaphoreType.DMA,
        ],
        compiler_params=pltpu.CompilerParams(vmem_limit_bytes=(2 << 20) + members * (1 << 19)),
        cost_estimate=pl.CostEstimate(
            flops=members * 2_000_000, bytes_accessed=members << 18, transcendentals=0
        ),
        name="turn",
    )(pieces)


def add_pairs(devices, first, base, count, list_ref, x_ref, sums_ref):
    def add(place, carry):
        code = list_ref[base + place]
        i, j = lax.div(code, devices), lax.rem(code, devices) - first
        scale = x_ref[j, ROWS : ROWS + 1, :].astype(jnp.float32)
        sums_ref[i] = sums_ref[i] + x_ref[j, 0:ROWS, :].astype(jnp.float32) * scale
        return carry

    lax.fori_loop(0, count, add, 0)


def middle_kernel(devices, list_ref, near_hbm, side_hbm, turned_y_ref, turned_s_ref, sums_ref, x_ref, high_ref, low_ref, sem):
    members = devices // GROUPS
    copies = [
        pltpu.make_async_copy(near_hbm, x_ref.at[pl.ds(0, 2 * members)], sem.at[0]),
        pltpu.make_async_copy(side_hbm, x_ref.at[pl.ds(2 * members, members)], sem.at[1]),
    ]
    for copy in copies:
        copy.start()
    sums_ref[...] = jnp.zeros_like(sums_ref)
    for copy in copies:
        copy.wait()
    for turned_ref, base in ((turned_y_ref, members), (turned_s_ref, 2 * members)):
        turn_group(
            lambda i, a, b, base=base: x_ref[base + i, a:b, :].astype(jnp.float32),
            members,
            turned_ref,
            high_ref,
            low_ref,
        )
    add_pairs(devices, 0, 2, list_ref[0], list_ref, x_ref, sums_ref)


def middle(devices, pairs, near, side):
    members = devices // GROUPS
    turned = jax.ShapeDtypeStruct((2 * LANES, members * ROWS), jnp.bfloat16)
    return pl.pallas_call(
        functools.partial(middle_kernel, devices),
        out_shape=(turned, turned, jax.ShapeDtypeStruct((devices, ROWS, LANES), jnp.float32)),
        in_specs=[SMEM, ANY, ANY],
        out_specs=(VMEM, VMEM, VMEM),
        scratch_shapes=[
            pltpu.VMEM((3 * members, HEAD, LANES), jnp.bfloat16),
            pltpu.VMEM((members * ROWS, LANES), jnp.bfloat16),
            pltpu.VMEM((members * ROWS, LANES), jnp.bfloat16),
            pltpu.SemaphoreType.DMA((2,)),
        ],
        compiler_params=pltpu.CompilerParams(vmem_limit_bytes=(2 << 20) + devices * (1 << 19)),
        cost_estimate=pl.CostEstimate(
            flops=devices * 2_000_000, bytes_accessed=devices << 18, transcendentals=0
        ),
        name="middle",
    )(pairs, near, side)


def stack_kernel(
    devices, span, list_ref, t0_ref, t1_ref, t2_ref, sums_hbm, last_hbm, out_ref,
    x_ref, sums_ref, a0_ref, a1_ref, a2_ref, a3_ref, high_ref, low_ref, yh_ref, yl_ref, sem,
):
    members = devices // GROUPS
    depth = members * ROWS
    slab = members * COARSE
    copies = [
        pltpu.make_async_copy(last_hbm, x_ref, sem.at[0]),
        pltpu.make_async_copy(sums_hbm, sums_ref, sem.at[1]),
        pltpu.make_async_copy(t0_ref, a0_ref, sem.at[2]),
        pltpu.make_async_copy(t1_ref, a1_ref, sem.at[3]),
        pltpu.make_async_copy(t2_ref, a2_ref, sem.at[4]),
    ]
    for copy in copies:
        copy.start()
    copies[0].wait()
    copies[1].wait()
    late_at = 3 + devices * devices
    add_pairs(devices, 3 * members, late_at, list_ref[1], list_ref, x_ref, sums_ref)
    for copy in copies[2:]:
        copy.wait()
    turn_group(loader(x_ref), members, a3_ref, high_ref, low_ref)

    def put(group, member, u1, value):
        high, low = split(value)
        at = ((u1 + REACH) * members + member) * COARSE
        yh_ref[group, at : at + COARSE, :] = high
        yl_ref[group, at : at + COARSE, :] = low

    products = [None] * SHIFTS
    for group, turned_ref in enumerate((a0_ref, a1_ref, a2_ref, a3_ref)):
        for member in range(members):
            total = sums_ref[group * members + member]
            parts = [total[u1 * COARSE : (u1 + 1) * COARSE] for u1 in range(FINE)]
            for u1 in range(FINE):
                put(group, member, u1, parts[u1])
            for u1 in range(REACH):
                put(group, member, u1 + FINE, pltpu.roll(parts[u1], COARSE - 1, 0))
            for u1 in range(FINE - REACH, FINE):
                put(group, member, u1 - FINE, pltpu.roll(parts[u1], 1, 0))
        for j in range(SHIFTS):
            both = jnp.dot(
                turned_ref[...],
                yh_ref[group, j * slab : j * slab + depth, :],
                preferred_element_type=jnp.float32,
            )
            rest = jnp.dot(
                turned_ref[0:LANES, :],
                yl_ref[group, j * slab : j * slab + depth, :],
                preferred_element_type=jnp.float32,
            )
            part = both[0:LANES] + both[LANES : 2 * LANES] + rest
            products[j] = part if group == 0 else products[j] + part
    product = jnp.concatenate(products, axis=1)
    stack = jnp.zeros((CH, OUT_LANES), jnp.float32)
    for v in range(STEP):
        stack = stack + product[CH * v : CH * (v + 1), CH * v : CH * v + OUT_LANES]
    count = (list_ref[0] + list_ref[1]).astype(jnp.float32)
    stack = stack / jnp.sqrt(jnp.full((CH, OUT_LANES), count * span, jnp.float32))
    for a in range(CH):
        out_ref[0:1, a * OUT_LANES : (a + 1) * OUT_LANES] = stack[a : a + 1]


def stack_bin(devices, span, pairs, turned, sums, last):
    members = devices // GROUPS
    depth = members * ROWS
    extended = members * COARSE * (FINE + 2 * REACH)
    left = pltpu.VMEM((2 * LANES, depth), jnp.bfloat16)
    return pl.pallas_call(
        functools.partial(stack_kernel, devices, float(span)),
        out_shape=jax.ShapeDtypeStruct((1, CH * OUT_LANES), jnp.float32),
        in_specs=[SMEM] + [ANY] * 5,
        out_specs=VMEM,
        scratch_shapes=[
            pltpu.VMEM((members, HEAD, LANES), jnp.bfloat16),
            pltpu.VMEM((devices, ROWS, LANES), jnp.float32),
            left,
            left,
            left,
            left,
            pltpu.VMEM((depth, LANES), jnp.bfloat16),
            pltpu.VMEM((depth, LANES), jnp.bfloat16),
            pltpu.VMEM((GROUPS, extended, LANES), jnp.bfloat16),
            pltpu.VMEM((GROUPS, extended, LANES), jnp.bfloat16),
            pltpu.SemaphoreType.DMA((5,)),
        ],
        compiler_params=pltpu.CompilerParams(vmem_limit_bytes=(8 << 20) + devices * (5 << 17)),
        name="stack",
    )(pairs, *turned, sums, last)


def on_device(samples, scales, bin_ids, owner_table):
    devices = lax.axis_size("chan")
    span = samples.shape[1] - 2 * LAG
    own = lax.axis_index("chan").reshape(1).astype(jnp.int32)

    def swap(value, offset):
        return lax.ppermute(value, "chan", [(i, i ^ offset) for i in range(devices)])

    piece = prep(samples, scales)
    pairs = find_pairs(devices, own, bin_ids, owner_table)
    members = devices // GROUPS
    near = jnp.zeros((2 * members,) + piece.shape, piece.dtype)
    near = near.at[0].set(piece)
    column = [piece]
    plane = [swap(piece, 2)]
    for i in range(1, members):
        one = swap(piece, 4 * i)
        column.append(one)
        plane.append(swap(one, 2))
        near = near.at[i].set(one)
    for i, one in enumerate(plane):
        near = near.at[members + i].set(one)
    own_column = jnp.stack(column)
    side_column = swap(own_column, 1)
    side_plane = swap(jnp.stack(plane), 1)
    turned_0 = turn(own_column)
    turned_1, turned_2, sums = middle(devices, pairs, near, side_column)
    return stack_bin(
        devices, span, pairs, (turned_0, turned_1, turned_2), sums, side_plane
    )


def solution(mesh):
    placed = (P(("groups", "chan"), None), P(("groups", "chan")), P(), P())
    return jax.shard_map(
        on_device,
        mesh=mesh,
        in_specs=placed,
        out_specs=P(("groups", "chan"), None),
        check_vma=False,
    )
```

```python
import functools

import jax
import jax.numpy as jnp
from jax import lax
from jax.experimental import pallas as pl
from jax.experimental.pallas import tpu as pltpu
from jax.sharding import PartitionSpec as P

LAG = 32
LAGS = 65
CH = 16
STEP = 16
LANES = CH * STEP
FINE = 8
COARSE = 16
ROWS = FINE * COARSE
HEAD = ROWS + 8
REACH = LAG // STEP
SHIFTS = 2 * REACH + 1
OUT_LANES = LAGS * CH
GROUPS = 4

VMEM = pl.BlockSpec(memory_space=pltpu.VMEM)
SMEM = pl.BlockSpec(memory_space=pltpu.SMEM)
ANY = pl.BlockSpec(memory_space=pl.ANY)
HBM = pl.BlockSpec(memory_space=pltpu.HBM)


def piece_offset(devices, index):
    far = devices // GROUPS
    return (
        lax.rem(index, far) * 4 + lax.rem(lax.div(index, far), 2) * 2 + lax.div(index, 2 * far)
    )


def prep_kernel(samples_ref, scales_ref, piece_ref, x_ref, s_ref, turned_ref, sem):
    copies = [
        pltpu.make_async_copy(samples_ref, x_ref, sem.at[0]),
        pltpu.make_async_copy(scales_ref, s_ref, sem.at[1]),
    ]
    for copy in copies:
        copy.start()
    copies[0].wait()
    samples = x_ref[...].astype(jnp.float32)
    for u2 in range(COARSE):
        turned_ref[u2 * 128 : (u2 + 1) * 128, 0:CH] = samples[:, u2 * 128 : (u2 + 1) * 128].T
    for u1 in range(FINE):
        parts = [
            turned_ref[pl.ds(STEP * u1 + v, COARSE, stride=128), 0:CH] for v in range(STEP)
        ]
        piece_ref[u1 * COARSE : (u1 + 1) * COARSE, :] = jnp.concatenate(parts, axis=1).astype(
            jnp.bfloat16
        )
    copies[1].wait()
    scales = s_ref[...].astype(jnp.float32)
    piece_ref[ROWS:HEAD, :] = jnp.broadcast_to(
        jnp.concatenate([scales] * STEP, axis=1), (HEAD - ROWS, LANES)
    ).astype(jnp.bfloat16)


def prep(samples, scales):
    return pl.pallas_call(
        prep_kernel,
        out_shape=jax.ShapeDtypeStruct((HEAD, LANES), jnp.bfloat16),
        in_specs=[HBM, HBM],
        out_specs=VMEM,
        scratch_shapes=[
            pltpu.VMEM(samples.shape, jnp.bfloat16),
            pltpu.VMEM((1, CH), jnp.bfloat16),
            pltpu.VMEM((COARSE * 128, 128), jnp.float32),
            pltpu.SemaphoreType.DMA((2,)),
        ],
        compiler_params=pltpu.CompilerParams(vmem_limit_bytes=4 << 20),
        name="prep",
    )(
        pltpu.with_memory_space_constraint(samples, pltpu.HBM),
        pltpu.with_memory_space_constraint(scales.reshape(1, CH), pltpu.HBM),
    )


def pairs_kernel(devices, own_ref, bins_ref, owner_ref, list_ref):
    own = own_ref[0]
    members = devices // GROUPS
    own_bin = jnp.int32(0)
    for i in range(devices):
        own_bin = jnp.where(owner_ref[i] == own, i, own_bin)

    def row(i, found):
        found = list(found)
        p = own ^ piece_offset(devices, i)
        for j in range(devices):
            group = j // members
            q = own ^ piece_offset(devices, jnp.int32(j))
            list_ref[GROUPS + group * devices * members + found[group]] = i * devices + j
            found[group] = found[group] + jnp.where(bins_ref[p, q] == own_bin, 1, 0)
        return tuple(found)

    found = lax.fori_loop(0, devices, row, (jnp.int32(0),) * GROUPS)
    for group in range(GROUPS):
        list_ref[group] = found[group]


def find_pairs(devices, own, bin_ids, owner_table):
    return pl.pallas_call(
        functools.partial(pairs_kernel, devices),
        out_shape=jax.ShapeDtypeStruct((GROUPS + devices * devices + 1,), jnp.int32),
        in_specs=[SMEM] * 3,
        out_specs=SMEM,
        compiler_params=pltpu.CompilerParams(vmem_limit_bytes=1 << 20),
        cost_estimate=pl.CostEstimate(flops=10_000_000, bytes_accessed=1 << 20, transcendentals=0),
        name="pairs",
    )(
        own,
        pltpu.with_memory_space_constraint(bin_ids, pltpu.HBM),
        pltpu.with_memory_space_constraint(owner_table, pltpu.HBM),
    )


def split(value):
    high = value.astype(jnp.bfloat16)
    return high, (value - high.astype(jnp.float32)).astype(jnp.bfloat16)


def inside_rows():
    row = lax.broadcasted_iota(jnp.int32, (ROWS, LANES), 0)
    u = FINE * (row % COARSE) + row // COARSE
    return (u >= REACH) & (u < ROWS - REACH)


def turn_group(load, members, turned_ref, high_ref, low_ref):
    inside = inside_rows()
    for i in range(members):
        scale = load(i, ROWS, ROWS + 1)
        high, low = split(jnp.where(inside, load(i, 0, ROWS) * scale, 0.0))
        for u1 in range(FINE):
            at = (u1 * members + i) * COARSE
            high_ref[at : at + COARSE, :] = high[u1 * COARSE : (u1 + 1) * COARSE]
            low_ref[at : at + COARSE, :] = low[u1 * COARSE : (u1 + 1) * COARSE]
    for k in range(0, members * ROWS, 128):
        turned_ref[0:LANES, k : k + 128] = high_ref[k : k + 128, :].T
        turned_ref[LANES : 2 * LANES, k : k + 128] = low_ref[k : k + 128, :].T


def loader(ref):
    return lambda i, start, stop: ref[i, start:stop, :].astype(jnp.float32)


def turn_kernel(x_ref, turned_ref, high_ref, low_ref):
    turn_group(loader(x_ref), x_ref.shape[0], turned_ref, high_ref, low_ref)


def turn(pieces):
    members = pieces.shape[0]
    return pl.pallas_call(
        turn_kernel,
        out_shape=jax.ShapeDtypeStruct((2 * LANES, members * ROWS), jnp.bfloat16),
        in_specs=[VMEM],
        out_specs=VMEM,
        scratch_shapes=[
            pltpu.VMEM((members * ROWS, LANES), jnp.bfloat16),
            pltpu.VMEM((members * ROWS, LANES), jnp.bfloat16),
        ],
        compiler_params=pltpu.CompilerParams(vmem_limit_bytes=(2 << 20) + members * (1 << 19)),
        cost_estimate=pl.CostEstimate(
            flops=members * 2_000_000, bytes_accessed=members << 18, transcendentals=0
        ),
        name="turn",
    )(pieces)


def add_pairs(devices, first, base, start, stop, list_ref, x_ref, sums_ref):
    def add(place, carry):
        code = list_ref[base + place]
        i, j = lax.div(code, devices), lax.rem(code, devices) - first
        scale = x_ref[j, ROWS : ROWS + 1, :].astype(jnp.float32)
        sums_ref[i] = sums_ref[i] + x_ref[j, 0:ROWS, :].astype(jnp.float32) * scale
        return carry

    lax.fori_loop(start, stop, add, 0)


def middle_kernel(
    devices, list_ref, column_ref, plane_ref, side_ref,
    turned_y_ref, turned_s_ref, sums_ref, high_ref, low_ref,
):
    members = devices // GROUPS
    sums_ref[...] = jnp.zeros_like(sums_ref)
    turn_group(loader(plane_ref), members, turned_y_ref, high_ref, low_ref)
    turn_group(loader(side_ref), members, turned_s_ref, high_ref, low_ref)
    for group, ref in enumerate((column_ref, plane_ref, side_ref)):
        base = GROUPS + group * devices * members
        add_pairs(devices, group * members, base, 0, list_ref[group], list_ref, ref, sums_ref)


def middle(devices, pairs, column, plane, side):
    members = devices // GROUPS
    turned = jax.ShapeDtypeStruct((2 * LANES, members * ROWS), jnp.bfloat16)
    return pl.pallas_call(
        functools.partial(middle_kernel, devices),
        out_shape=(turned, turned, jax.ShapeDtypeStruct((devices, ROWS, LANES), jnp.float32)),
        in_specs=[SMEM, VMEM, VMEM, VMEM],
        out_specs=(VMEM, VMEM, VMEM),
        scratch_shapes=[
            pltpu.VMEM((members * ROWS, LANES), jnp.bfloat16),
            pltpu.VMEM((members * ROWS, LANES), jnp.bfloat16),
        ],
        compiler_params=pltpu.CompilerParams(vmem_limit_bytes=(2 << 20) + devices * (1 << 19)),
        cost_estimate=pl.CostEstimate(
            flops=devices * 2_000_000, bytes_accessed=devices << 18, transcendentals=0
        ),
        name="middle",
    )(pairs, column, plane, side)


def stack_kernel(
    devices, span, list_ref, a0_ref, a1_ref, a2_ref, _, x_ref, out_ref, sums_ref,
    a3_ref, high_ref, low_ref, yh_ref, yl_ref,
):
    members = devices // GROUPS
    depth = members * ROWS
    slab = members * COARSE
    last = GROUPS - 1
    base = GROUPS + last * devices * members
    add_pairs(devices, last * members, base, 0, list_ref[last], list_ref, x_ref, sums_ref)
    turn_group(loader(x_ref), members, a3_ref, high_ref, low_ref)

    def put(group, member, u1, value):
        high, low = split(value)
        at = ((u1 + REACH) * members + member) * COARSE
        yh_ref[group, at : at + COARSE, :] = high
        yl_ref[group, at : at + COARSE, :] = low

    products = [None] * SHIFTS
    for group, turned_ref in enumerate((a0_ref, a1_ref, a2_ref, a3_ref)):
        for member in range(members):
            total = sums_ref[group * members + member]
            parts = [total[u1 * COARSE : (u1 + 1) * COARSE] for u1 in range(FINE)]
            for u1 in range(FINE):
                put(group, member, u1, parts[u1])
            for u1 in range(REACH):
                put(group, member, u1 + FINE, pltpu.roll(parts[u1], COARSE - 1, 0))
            for u1 in range(FINE - REACH, FINE):
                put(group, member, u1 - FINE, pltpu.roll(parts[u1], 1, 0))
        for j in range(SHIFTS):
            both = jnp.dot(
                turned_ref[...],
                yh_ref[group, j * slab : j * slab + depth, :],
                preferred_element_type=jnp.float32,
            )
            rest = jnp.dot(
                turned_ref[0:LANES, :],
                yl_ref[group, j * slab : j * slab + depth, :],
                preferred_element_type=jnp.float32,
            )
            part = both[0:LANES] + both[LANES : 2 * LANES] + rest
            products[j] = part if group == 0 else products[j] + part
    product = jnp.concatenate(products, axis=1)
    stack = jnp.zeros((CH, OUT_LANES), jnp.float32)
    for v in range(STEP):
        stack = stack + product[CH * v : CH * (v + 1), CH * v : CH * v + OUT_LANES]
    count = sum(list_ref[group] for group in range(GROUPS)).astype(jnp.float32)
    stack = stack / jnp.sqrt(jnp.full((CH, OUT_LANES), count * span, jnp.float32))
    for a in range(CH):
        out_ref[0:1, a * OUT_LANES : (a + 1) * OUT_LANES] = stack[a : a + 1]


def stack_bin(devices, span, pairs, turned, sums, last):
    members = devices // GROUPS
    depth = members * ROWS
    extended = members * COARSE * (FINE + 2 * REACH)
    stack, _ = pl.pallas_call(
        functools.partial(stack_kernel, devices, float(span)),
        out_shape=(
            jax.ShapeDtypeStruct((1, CH * OUT_LANES), jnp.float32),
            jax.ShapeDtypeStruct(sums.shape, jnp.float32),
        ),
        in_specs=[SMEM] + [VMEM] * 5,
        out_specs=(VMEM, VMEM),
        input_output_aliases={4: 1},
        scratch_shapes=[
            pltpu.VMEM((2 * LANES, depth), jnp.bfloat16),
            pltpu.VMEM((depth, LANES), jnp.bfloat16),
            pltpu.VMEM((depth, LANES), jnp.bfloat16),
            pltpu.VMEM((GROUPS, extended, LANES), jnp.bfloat16),
            pltpu.VMEM((GROUPS, extended, LANES), jnp.bfloat16),
        ],
        compiler_params=pltpu.CompilerParams(vmem_limit_bytes=(8 << 20) + devices * (5 << 17)),
        name="stack",
    )(pairs, *turned, sums, last)
    return stack


def on_device(samples, scales, bin_ids, owner_table):
    devices = lax.axis_size("chan")
    span = samples.shape[1] - 2 * LAG
    own = lax.axis_index("chan").reshape(1).astype(jnp.int32)

    def swap(value, offset):
        return lax.ppermute(value, "chan", [(i, i ^ offset) for i in range(devices)])

    piece = prep(samples, scales)
    pairs = find_pairs(devices, own, bin_ids, owner_table)
    members = devices // GROUPS
    own_column = jnp.zeros((members,) + piece.shape, piece.dtype).at[0].set(piece)
    plane = [swap(piece, 2)]
    for i in range(1, members):
        one = swap(piece, 4 * i)
        plane.append(swap(one, 2))
        own_column = own_column.at[i].set(one)
    side_column = swap(own_column, 1)
    own_plane = jnp.stack(plane)
    side_plane = swap(own_plane, 1)
    turned_0 = turn(own_column)
    turned_1, turned_2, sums = middle(devices, pairs, own_column, own_plane, side_column)
    return stack_bin(
        devices, span, pairs, (turned_0, turned_1, turned_2), sums, side_plane
    )


def solution(mesh):
    placed = (P(("groups", "chan"), None), P(("groups", "chan")), P(), P())
    return jax.shard_map(
        on_device,
        mesh=mesh,
        in_specs=placed,
        out_specs=P(("groups", "chan"), None),
        check_vma=False,
    )
```

```python
import functools

import jax
import jax.numpy as jnp
from jax import lax
from jax.experimental import pallas as pl
from jax.experimental.pallas import tpu as pltpu
from jax.sharding import PartitionSpec as P

LAG = 32
LAGS = 65
CH = 16
STEP = 16
LANES = CH * STEP
FINE = 8
COARSE = 16
ROWS = FINE * COARSE
HEAD = ROWS + 8
REACH = LAG // STEP
SHIFTS = 2 * REACH + 1
OUT_LANES = LAGS * CH
BLEND = 32.0
GROUPS = 4

VMEM = pl.BlockSpec(memory_space=pltpu.VMEM)
SMEM = pl.BlockSpec(memory_space=pltpu.SMEM)
ANY = pl.BlockSpec(memory_space=pl.ANY)
HBM = pl.BlockSpec(memory_space=pltpu.HBM)


def piece_offset(devices, index):
    far = devices // GROUPS
    return (
        lax.rem(index, far) * 4 + lax.rem(lax.div(index, far), 2) * 2 + lax.div(index, 2 * far)
    )


def prep_kernel(samples_ref, scales_ref, piece_ref, x_ref, s_ref, turned_ref, sem):
    copies = [
        pltpu.make_async_copy(samples_ref, x_ref, sem.at[0]),
        pltpu.make_async_copy(scales_ref, s_ref, sem.at[1]),
    ]
    for copy in copies:
        copy.start()
    copies[0].wait()
    samples = x_ref[...].astype(jnp.float32)
    for u2 in range(COARSE):
        turned_ref[u2 * 128 : (u2 + 1) * 128, 0:CH] = samples[:, u2 * 128 : (u2 + 1) * 128].T
    for u1 in range(FINE):
        parts = [
            turned_ref[pl.ds(STEP * u1 + v, COARSE, stride=128), 0:CH] for v in range(STEP)
        ]
        piece_ref[u1 * COARSE : (u1 + 1) * COARSE, :] = jnp.concatenate(parts, axis=1).astype(
            jnp.bfloat16
        )
    copies[1].wait()
    scales = s_ref[...].astype(jnp.float32)
    piece_ref[ROWS:HEAD, :] = jnp.broadcast_to(
        jnp.concatenate([scales] * STEP, axis=1), (HEAD - ROWS, LANES)
    ).astype(jnp.bfloat16)


def prep(samples, scales):
    return pl.pallas_call(
        prep_kernel,
        out_shape=jax.ShapeDtypeStruct((HEAD, LANES), jnp.bfloat16),
        in_specs=[HBM, HBM],
        out_specs=VMEM,
        scratch_shapes=[
            pltpu.VMEM(samples.shape, jnp.bfloat16),
            pltpu.VMEM((1, CH), jnp.bfloat16),
            pltpu.VMEM((COARSE * 128, 128), jnp.float32),
            pltpu.SemaphoreType.DMA((2,)),
        ],
        compiler_params=pltpu.CompilerParams(vmem_limit_bytes=4 << 20),
        name="prep",
    )(
        pltpu.with_memory_space_constraint(samples, pltpu.HBM),
        pltpu.with_memory_space_constraint(scales.reshape(1, CH), pltpu.HBM),
    )


def pairs_kernel(devices, own_ref, bins_ref, owner_ref, list_ref):
    own = own_ref[0]
    members = devices // GROUPS
    own_bin = jnp.int32(0)
    for i in range(devices):
        own_bin = jnp.where(owner_ref[i] == own, i, own_bin)

    def row(i, found):
        found = list(found)
        p = own ^ piece_offset(devices, i)
        for j in range(devices):
            group = j // members
            q = own ^ piece_offset(devices, jnp.int32(j))
            list_ref[GROUPS + group * devices * members + found[group]] = i * devices + j
            found[group] = found[group] + jnp.where(bins_ref[p, q] == own_bin, 1, 0)
        return tuple(found)

    found = lax.fori_loop(0, devices, row, (jnp.int32(0),) * GROUPS)
    for group in range(GROUPS):
        list_ref[group] = found[group]


def find_pairs(devices, own, bin_ids, owner_table):
    return pl.pallas_call(
        functools.partial(pairs_kernel, devices),
        out_shape=jax.ShapeDtypeStruct((GROUPS + devices * devices + 1,), jnp.int32),
        in_specs=[SMEM] * 3,
        out_specs=SMEM,
        compiler_params=pltpu.CompilerParams(vmem_limit_bytes=1 << 20),
        cost_estimate=pl.CostEstimate(flops=10_000_000, bytes_accessed=1 << 20, transcendentals=0),
        name="pairs",
    )(
        own,
        pltpu.with_memory_space_constraint(bin_ids, pltpu.HBM),
        pltpu.with_memory_space_constraint(owner_table, pltpu.HBM),
    )


def split_left(value):
    high = value.astype(jnp.bfloat16)
    wide = high.astype(jnp.float32)
    return high, (wide + BLEND * (value - wide)).astype(jnp.bfloat16)


def split_right(value):
    high = value.astype(jnp.bfloat16)
    wide = high.astype(jnp.float32)
    return high, (wide * (1.0 / BLEND) + (value - wide)).astype(jnp.bfloat16)


def inside_rows():
    row = lax.broadcasted_iota(jnp.int32, (ROWS, LANES), 0)
    u = FINE * (row % COARSE) + row // COARSE
    return (u >= REACH) & (u < ROWS - REACH)


def turn_group(load, members, turned_ref, high_ref, low_ref):
    inside = inside_rows()
    for i in range(members):
        scale = load(i, ROWS, ROWS + 1)
        high, low = split_left(jnp.where(inside, load(i, 0, ROWS) * scale, 0.0))
        for u1 in range(FINE):
            at = (u1 * members + i) * COARSE
            high_ref[at : at + COARSE, :] = high[u1 * COARSE : (u1 + 1) * COARSE]
            low_ref[at : at + COARSE, :] = low[u1 * COARSE : (u1 + 1) * COARSE]
    for k in range(0, members * ROWS, 128):
        turned_ref[0:LANES, k : k + 128] = high_ref[k : k + 128, :].T
        turned_ref[LANES : 2 * LANES, k : k + 128] = low_ref[k : k + 128, :].T


def loader(ref):
    return lambda i, start, stop: ref[i, start:stop, :].astype(jnp.float32)


def turn_kernel(x_ref, turned_ref, high_ref, low_ref):
    turn_group(loader(x_ref), x_ref.shape[0], turned_ref, high_ref, low_ref)


def turn(pieces):
    members = pieces.shape[0]
    return pl.pallas_call(
        turn_kernel,
        out_shape=jax.ShapeDtypeStruct((2 * LANES, members * ROWS), jnp.bfloat16),
        in_specs=[VMEM],
        out_specs=VMEM,
        scratch_shapes=[
            pltpu.VMEM((members * ROWS, LANES), jnp.bfloat16),
            pltpu.VMEM((members * ROWS, LANES), jnp.bfloat16),
        ],
        compiler_params=pltpu.CompilerParams(vmem_limit_bytes=(2 << 20) + members * (1 << 19)),
        cost_estimate=pl.CostEstimate(
            flops=members * 2_000_000, bytes_accessed=members << 18, transcendentals=0
        ),
        name="turn",
    )(pieces)


def add_pairs(devices, first, base, start, stop, list_ref, x_ref, sums_ref):
    def add(place, carry):
        code = list_ref[base + place]
        i, j = lax.div(code, devices), lax.rem(code, devices) - first
        scale = x_ref[j, ROWS : ROWS + 1, :].astype(jnp.float32)
        sums_ref[i] = sums_ref[i] + x_ref[j, 0:ROWS, :].astype(jnp.float32) * scale
        return carry

    lax.fori_loop(start, stop, add, 0)


def early_kernel(devices, list_ref, column_ref, side_ref, turned_ref, sums_ref, high_ref, low_ref):
    members = devices // GROUPS
    sums_ref[...] = jnp.zeros_like(sums_ref)
    turn_group(loader(side_ref), members, turned_ref, high_ref, low_ref)
    for group, ref in ((0, column_ref), (2, side_ref)):
        base = GROUPS + group * devices * members
        add_pairs(devices, group * members, base, 0, list_ref[group], list_ref, ref, sums_ref)


def plane_kernel(devices, list_ref, plane_ref, _, turned_ref, sums_ref, high_ref, low_ref):
    members = devices // GROUPS
    turn_group(loader(plane_ref), members, turned_ref, high_ref, low_ref)
    base = GROUPS + devices * members
    add_pairs(devices, members, base, 0, list_ref[1], list_ref, plane_ref, sums_ref)


def early(devices, pairs, column, side):
    members = devices // GROUPS
    return pl.pallas_call(
        functools.partial(early_kernel, devices),
        out_shape=(
            jax.ShapeDtypeStruct((2 * LANES, members * ROWS), jnp.bfloat16),
            jax.ShapeDtypeStruct((devices, ROWS, LANES), jnp.float32),
        ),
        in_specs=[SMEM, VMEM, VMEM],
        out_specs=(VMEM, VMEM),
        scratch_shapes=[
            pltpu.VMEM((members * ROWS, LANES), jnp.bfloat16),
            pltpu.VMEM((members * ROWS, LANES), jnp.bfloat16),
        ],
        compiler_params=pltpu.CompilerParams(vmem_limit_bytes=(2 << 20) + devices * (1 << 19)),
        cost_estimate=pl.CostEstimate(
            flops=devices * 2_000_000, bytes_accessed=devices << 18, transcendentals=0
        ),
        name="early",
    )(pairs, column, side)


def add_plane(devices, pairs, plane, sums):
    members = devices // GROUPS
    return pl.pallas_call(
        functools.partial(plane_kernel, devices),
        out_shape=(
            jax.ShapeDtypeStruct((2 * LANES, members * ROWS), jnp.bfloat16),
            jax.ShapeDtypeStruct(sums.shape, jnp.float32),
        ),
        in_specs=[SMEM, VMEM, VMEM],
        out_specs=(VMEM, VMEM),
        input_output_aliases={2: 1},
        scratch_shapes=[
            pltpu.VMEM((members * ROWS, LANES), jnp.bfloat16),
            pltpu.VMEM((members * ROWS, LANES), jnp.bfloat16),
        ],
        compiler_params=pltpu.CompilerParams(vmem_limit_bytes=(2 << 20) + devices * (1 << 19)),
        cost_estimate=pl.CostEstimate(
            flops=devices * 1_000_000, bytes_accessed=devices << 17, transcendentals=0
        ),
        name="plane",
    )(pairs, plane, sums)


def stack_kernel(
    devices, span, list_ref, a0_ref, a1_ref, a2_ref, _, x_ref, out_ref, sums_ref,
    a3_ref, high_ref, low_ref, yh_ref, yl_ref,
):
    members = devices // GROUPS
    depth = members * ROWS
    slab = members * COARSE
    last = GROUPS - 1
    base = GROUPS + last * devices * members
    add_pairs(devices, last * members, base, 0, list_ref[last], list_ref, x_ref, sums_ref)
    turn_group(loader(x_ref), members, a3_ref, high_ref, low_ref)

    def put(group, member, u1, value):
        high, low = split_right(value)
        at = ((u1 + REACH) * members + member) * COARSE
        yh_ref[group, at : at + COARSE, :] = high
        yl_ref[group, at : at + COARSE, :] = low

    products = [None] * SHIFTS
    for group, turned_ref in enumerate((a0_ref, a1_ref, a2_ref, a3_ref)):
        for member in range(members):
            total = sums_ref[group * members + member]
            parts = [total[u1 * COARSE : (u1 + 1) * COARSE] for u1 in range(FINE)]
            for u1 in range(FINE):
                put(group, member, u1, parts[u1])
            for u1 in range(REACH):
                put(group, member, u1 + FINE, pltpu.roll(parts[u1], COARSE - 1, 0))
            for u1 in range(FINE - REACH, FINE):
                put(group, member, u1 - FINE, pltpu.roll(parts[u1], 1, 0))
        for j in range(SHIFTS):
            rows = slice(j * slab, j * slab + depth)
            main = jnp.dot(
                turned_ref[0:LANES, :], yh_ref[group, rows, :], preferred_element_type=jnp.float32
            )
            rest = jnp.dot(
                turned_ref[LANES : 2 * LANES, :],
                yl_ref[group, rows, :],
                preferred_element_type=jnp.float32,
            )
            part = main * (1.0 - 1.0 / BLEND) + rest
            products[j] = part if group == 0 else products[j] + part
    product = jnp.concatenate(products, axis=1)
    stack = jnp.zeros((CH, OUT_LANES), jnp.float32)
    for v in range(STEP):
        stack = stack + product[CH * v : CH * (v + 1), CH * v : CH * v + OUT_LANES]
    count = sum(list_ref[group] for group in range(GROUPS)).astype(jnp.float32)
    stack = stack / jnp.sqrt(jnp.full((CH, OUT_LANES), count * span, jnp.float32))
    for a in range(CH):
        out_ref[0:1, a * OUT_LANES : (a + 1) * OUT_LANES] = stack[a : a + 1]


def stack_bin(devices, span, pairs, turned, sums, last):
    members = devices // GROUPS
    depth = members * ROWS
    extended = members * COARSE * (FINE + 2 * REACH)
    stack, _ = pl.pallas_call(
        functools.partial(stack_kernel, devices, float(span)),
        out_shape=(
            jax.ShapeDtypeStruct((1, CH * OUT_LANES), jnp.float32),
            jax.ShapeDtypeStruct(sums.shape, jnp.float32),
        ),
        in_specs=[SMEM] + [VMEM] * 5,
        out_specs=(VMEM, VMEM),
        input_output_aliases={4: 1},
        scratch_shapes=[
            pltpu.VMEM((2 * LANES, depth), jnp.bfloat16),
            pltpu.VMEM((depth, LANES), jnp.bfloat16),
            pltpu.VMEM((depth, LANES), jnp.bfloat16),
            pltpu.VMEM((GROUPS, extended, LANES), jnp.bfloat16),
            pltpu.VMEM((GROUPS, extended, LANES), jnp.bfloat16),
        ],
        compiler_params=pltpu.CompilerParams(vmem_limit_bytes=(8 << 20) + devices * (5 << 17)),
        name="stack",
    )(pairs, *turned, sums, last)
    return stack


def on_device(samples, scales, bin_ids, owner_table):
    devices = lax.axis_size("chan")
    span = samples.shape[1] - 2 * LAG
    own = lax.axis_index("chan").reshape(1).astype(jnp.int32)

    def swap(value, offset):
        return lax.ppermute(value, "chan", [(i, i ^ offset) for i in range(devices)])

    piece = prep(samples, scales)
    pairs = find_pairs(devices, own, bin_ids, owner_table)
    members = devices // GROUPS
    own_column = jnp.zeros((members,) + piece.shape, piece.dtype).at[0].set(piece)
    plane = [swap(piece, 2)]
    for i in range(1, members):
        one = swap(piece, 4 * i)
        plane.append(swap(one, 2))
        own_column = own_column.at[i].set(one)
    side_column = swap(own_column, 1)
    own_plane = jnp.stack(plane)
    side_plane = swap(own_plane, 1)
    turned_0 = turn(own_column)
    turned_2, sums = early(devices, pairs, own_column, side_column)
    turned_1, sums = add_plane(devices, pairs, own_plane, sums)
    return stack_bin(
        devices, span, pairs, (turned_0, turned_1, turned_2), sums, side_plane
    )


def solution(mesh):
    placed = (P(("groups", "chan"), None), P(("groups", "chan")), P(), P())
    return jax.shard_map(
        on_device,
        mesh=mesh,
        in_specs=placed,
        out_specs=P(("groups", "chan"), None),
        check_vma=False,
    )
```

```python
import functools

import jax
import jax.numpy as jnp
from jax import lax
from jax.experimental import pallas as pl
from jax.experimental.pallas import tpu as pltpu
from jax.sharding import PartitionSpec as P

LAG = 32
LAGS = 65
CH = 16
STEP = 16
LANES = CH * STEP
FINE = 8
COARSE = 16
ROWS = FINE * COARSE
HEAD = ROWS + 8
REACH = LAG // STEP
SHIFTS = 2 * REACH + 1
OUT_LANES = LAGS * CH
BLEND = 32.0
HEADER = 8
GROUPS = 4

VMEM = pl.BlockSpec(memory_space=pltpu.VMEM)
SMEM = pl.BlockSpec(memory_space=pltpu.SMEM)
ANY = pl.BlockSpec(memory_space=pl.ANY)
HBM = pl.BlockSpec(memory_space=pltpu.HBM)


def piece_index(devices, offset):
    bits = (devices // GROUPS).bit_length() - 1
    return (offset >> 2) | (((offset >> 1) & 1) << bits) | ((offset & 1) << (bits + 1))


def prep_kernel(samples_ref, scales_ref, piece_ref, x_ref, s_ref, turned_ref, sem):
    copies = [
        pltpu.make_async_copy(samples_ref, x_ref, sem.at[0]),
        pltpu.make_async_copy(scales_ref, s_ref, sem.at[1]),
    ]
    for copy in copies:
        copy.start()
    copies[0].wait()
    samples = x_ref[...].astype(jnp.float32)
    for u2 in range(COARSE):
        turned_ref[u2 * 128 : (u2 + 1) * 128, 0:CH] = samples[:, u2 * 128 : (u2 + 1) * 128].T
    for u1 in range(FINE):
        parts = [
            turned_ref[pl.ds(STEP * u1 + v, COARSE, stride=128), 0:CH] for v in range(STEP)
        ]
        piece_ref[u1 * COARSE : (u1 + 1) * COARSE, :] = jnp.concatenate(parts, axis=1).astype(
            jnp.bfloat16
        )
    copies[1].wait()
    scales = s_ref[...].astype(jnp.float32)
    piece_ref[ROWS:HEAD, :] = jnp.broadcast_to(
        jnp.concatenate([scales] * STEP, axis=1), (HEAD - ROWS, LANES)
    ).astype(jnp.bfloat16)


def prep(samples, scales):
    return pl.pallas_call(
        prep_kernel,
        out_shape=jax.ShapeDtypeStruct((HEAD, LANES), jnp.bfloat16),
        in_specs=[HBM, HBM],
        out_specs=VMEM,
        scratch_shapes=[
            pltpu.VMEM(samples.shape, jnp.bfloat16),
            pltpu.VMEM((1, CH), jnp.bfloat16),
            pltpu.VMEM((COARSE * 128, 128), jnp.float32),
            pltpu.SemaphoreType.DMA((2,)),
        ],
        compiler_params=pltpu.CompilerParams(vmem_limit_bytes=4 << 20),
        name="prep",
    )(
        pltpu.with_memory_space_constraint(samples, pltpu.HBM),
        pltpu.with_memory_space_constraint(scales.reshape(1, CH), pltpu.HBM),
    )


def pairs_kernel(devices, own_ref, bins_ref, owner_ref, list_ref):
    own = own_ref[0]
    members = devices // GROUPS
    own_bin = jnp.int32(0)
    for i in range(devices):
        own_bin = jnp.where(owner_ref[i] == own, i, own_bin)

    def row(p, found):
        found = list(found)
        cells = [bins_ref[p, q] for q in range(devices)]
        for q, cell in enumerate(cells):
            kind = q % GROUPS
            list_ref[HEADER + kind * devices * members + found[kind]] = p * members + q // GROUPS
            found[kind] = found[kind] + jnp.where(cell == own_bin, 1, 0)
        return tuple(found)

    found = lax.fori_loop(0, devices, row, (jnp.int32(0),) * GROUPS)
    list_ref[0] = own
    for kind in range(GROUPS):
        list_ref[1 + kind] = found[kind]


def find_pairs(devices, own, bin_ids, owner_table):
    return pl.pallas_call(
        functools.partial(pairs_kernel, devices),
        out_shape=jax.ShapeDtypeStruct((HEADER + devices * devices + 1,), jnp.int32),
        in_specs=[SMEM] * 3,
        out_specs=SMEM,
        compiler_params=pltpu.CompilerParams(vmem_limit_bytes=1 << 20),
        cost_estimate=pl.CostEstimate(flops=10_000_000, bytes_accessed=1 << 20, transcendentals=0),
        name="pairs",
    )(
        own,
        pltpu.with_memory_space_constraint(bin_ids, pltpu.HBM),
        pltpu.with_memory_space_constraint(owner_table, pltpu.HBM),
    )


def split_left(value):
    high = value.astype(jnp.bfloat16)
    wide = high.astype(jnp.float32)
    return high, (wide + BLEND * (value - wide)).astype(jnp.bfloat16)


def split_right(value):
    high = value.astype(jnp.bfloat16)
    wide = high.astype(jnp.float32)
    return high, (wide * (1.0 / BLEND) + (value - wide)).astype(jnp.bfloat16)


def inside_rows():
    row = lax.broadcasted_iota(jnp.int32, (ROWS, LANES), 0)
    u = FINE * (row % COARSE) + row // COARSE
    return (u >= REACH) & (u < ROWS - REACH)


def turn_group(load, members, turned_ref, high_ref, low_ref):
    inside = inside_rows()
    for i in range(members):
        scale = load(i, ROWS, ROWS + 1)
        high, low = split_left(jnp.where(inside, load(i, 0, ROWS) * scale, 0.0))
        for u1 in range(FINE):
            at = (u1 * members + i) * COARSE
            high_ref[at : at + COARSE, :] = high[u1 * COARSE : (u1 + 1) * COARSE]
            low_ref[at : at + COARSE, :] = low[u1 * COARSE : (u1 + 1) * COARSE]
    for k in range(0, members * ROWS, 128):
        turned_ref[0:LANES, k : k + 128] = high_ref[k : k + 128, :].T
        turned_ref[LANES : 2 * LANES, k : k + 128] = low_ref[k : k + 128, :].T


def loader(ref):
    return lambda i, start, stop: ref[i, start:stop, :].astype(jnp.float32)


def turn_kernel(x_ref, turned_ref, high_ref, low_ref):
    turn_group(loader(x_ref), x_ref.shape[0], turned_ref, high_ref, low_ref)


def turn(pieces):
    members = pieces.shape[0]
    return pl.pallas_call(
        turn_kernel,
        out_shape=jax.ShapeDtypeStruct((2 * LANES, members * ROWS), jnp.bfloat16),
        in_specs=[VMEM],
        out_specs=VMEM,
        scratch_shapes=[
            pltpu.VMEM((members * ROWS, LANES), jnp.bfloat16),
            pltpu.VMEM((members * ROWS, LANES), jnp.bfloat16),
        ],
        compiler_params=pltpu.CompilerParams(vmem_limit_bytes=(2 << 20) + members * (1 << 19)),
        cost_estimate=pl.CostEstimate(
            flops=members * 2_000_000, bytes_accessed=members << 18, transcendentals=0
        ),
        name="turn",
    )(pieces)


def add_pairs(devices, group, list_ref, x_ref, sums_ref):
    members = devices // GROUPS
    own = list_ref[0]
    kind = (own & 3) ^ (((group & 1) << 1) | (group >> 1))
    base = HEADER + kind * devices * members

    def add(place, carry):
        code = list_ref[base + place]
        i = piece_index(devices, own ^ (code >> (members.bit_length() - 1)))
        j = (code & (members - 1)) ^ (own >> 2)
        scale = x_ref[j, ROWS : ROWS + 1, :].astype(jnp.float32)
        sums_ref[i] = sums_ref[i] + x_ref[j, 0:ROWS, :].astype(jnp.float32) * scale
        return carry

    lax.fori_loop(0, list_ref[1 + kind], add, 0)


def early_kernel(
    devices, pairs_ref, column_ref, side_ref, turned_ref, sums_ref, list_ref, high_ref, low_ref, sem
):
    members = devices // GROUPS
    copy = pltpu.make_async_copy(pairs_ref, list_ref, sem)
    copy.start()
    sums_ref[...] = jnp.zeros_like(sums_ref)
    turn_group(loader(side_ref), members, turned_ref, high_ref, low_ref)
    copy.wait()
    for group, ref in ((0, column_ref), (2, side_ref)):
        add_pairs(devices, group, list_ref, ref, sums_ref)


def plane_kernel(
    devices, pairs_ref, plane_ref, _, turned_ref, sums_ref, list_ref, high_ref, low_ref, sem
):
    members = devices // GROUPS
    copy = pltpu.make_async_copy(pairs_ref, list_ref, sem)
    copy.start()
    turn_group(loader(plane_ref), members, turned_ref, high_ref, low_ref)
    copy.wait()
    add_pairs(devices, 1, list_ref, plane_ref, sums_ref)


def early(devices, pairs, column, side):
    members = devices // GROUPS
    return pl.pallas_call(
        functools.partial(early_kernel, devices),
        out_shape=(
            jax.ShapeDtypeStruct((2 * LANES, members * ROWS), jnp.bfloat16),
            jax.ShapeDtypeStruct((devices, ROWS, LANES), jnp.float32),
        ),
        in_specs=[ANY, VMEM, VMEM],
        out_specs=(VMEM, VMEM),
        scratch_shapes=[
            pltpu.SMEM(pairs.shape, jnp.int32),
            pltpu.VMEM((members * ROWS, LANES), jnp.bfloat16),
            pltpu.VMEM((members * ROWS, LANES), jnp.bfloat16),
            pltpu.SemaphoreType.DMA,
        ],
        compiler_params=pltpu.CompilerParams(vmem_limit_bytes=(2 << 20) + devices * (1 << 19)),
        cost_estimate=pl.CostEstimate(
            flops=devices * 2_000_000, bytes_accessed=devices << 18, transcendentals=0
        ),
        name="early",
    )(pairs, column, side)


def add_plane(devices, pairs, plane, sums):
    members = devices // GROUPS
    return pl.pallas_call(
        functools.partial(plane_kernel, devices),
        out_shape=(
            jax.ShapeDtypeStruct((2 * LANES, members * ROWS), jnp.bfloat16),
            jax.ShapeDtypeStruct(sums.shape, jnp.float32),
        ),
        in_specs=[ANY, VMEM, VMEM],
        out_specs=(VMEM, VMEM),
        input_output_aliases={2: 1},
        scratch_shapes=[
            pltpu.SMEM(pairs.shape, jnp.int32),
            pltpu.VMEM((members * ROWS, LANES), jnp.bfloat16),
            pltpu.VMEM((members * ROWS, LANES), jnp.bfloat16),
            pltpu.SemaphoreType.DMA,
        ],
        compiler_params=pltpu.CompilerParams(vmem_limit_bytes=(2 << 20) + devices * (1 << 19)),
        cost_estimate=pl.CostEstimate(
            flops=devices * 1_000_000, bytes_accessed=devices << 17, transcendentals=0
        ),
        name="plane",
    )(pairs, plane, sums)


def stack_kernel(
    devices, span, pairs_ref, a0_ref, a1_ref, a2_ref, _, x_ref, out_ref, sums_ref,
    list_ref, a3_ref, high_ref, low_ref, yh_ref, yl_ref, sem,
):
    members = devices // GROUPS
    depth = members * ROWS
    slab = members * COARSE
    copy = pltpu.make_async_copy(pairs_ref, list_ref, sem)
    copy.start()
    turn_group(loader(x_ref), members, a3_ref, high_ref, low_ref)
    copy.wait()
    add_pairs(devices, GROUPS - 1, list_ref, x_ref, sums_ref)

    def put(group, member, u1, value):
        high, low = split_right(value)
        at = ((u1 + REACH) * members + member) * COARSE
        yh_ref[group, at : at + COARSE, :] = high
        yl_ref[group, at : at + COARSE, :] = low

    products = [None] * SHIFTS
    for group, turned_ref in enumerate((a0_ref, a1_ref, a2_ref, a3_ref)):
        for member in range(members):
            total = sums_ref[group * members + member]
            parts = [total[u1 * COARSE : (u1 + 1) * COARSE] for u1 in range(FINE)]
            for u1 in range(FINE):
                put(group, member, u1, parts[u1])
            for u1 in range(REACH):
                put(group, member, u1 + FINE, pltpu.roll(parts[u1], COARSE - 1, 0))
            for u1 in range(FINE - REACH, FINE):
                put(group, member, u1 - FINE, pltpu.roll(parts[u1], 1, 0))
        for j in range(SHIFTS):
            rows = slice(j * slab, j * slab + depth)
            main = jnp.dot(
                turned_ref[0:LANES, :], yh_ref[group, rows, :], preferred_element_type=jnp.float32
            )
            rest = jnp.dot(
                turned_ref[LANES : 2 * LANES, :],
                yl_ref[group, rows, :],
                preferred_element_type=jnp.float32,
            )
            part = main * (1.0 - 1.0 / BLEND) + rest
            products[j] = part if group == 0 else products[j] + part
    product = jnp.concatenate(products, axis=1)
    stack = jnp.zeros((CH, OUT_LANES), jnp.float32)
    for v in range(STEP):
        stack = stack + product[CH * v : CH * (v + 1), CH * v : CH * v + OUT_LANES]
    count = sum(list_ref[1 + kind] for kind in range(GROUPS)).astype(jnp.float32)
    stack = stack / jnp.sqrt(jnp.full((CH, OUT_LANES), count * span, jnp.float32))
    for a in range(CH):
        out_ref[0:1, a * OUT_LANES : (a + 1) * OUT_LANES] = stack[a : a + 1]


def stack_bin(devices, span, pairs, turned, sums, last):
    members = devices // GROUPS
    depth = members * ROWS
    extended = members * COARSE * (FINE + 2 * REACH)
    stack, _ = pl.pallas_call(
        functools.partial(stack_kernel, devices, float(span)),
        out_shape=(
            jax.ShapeDtypeStruct((1, CH * OUT_LANES), jnp.float32),
            jax.ShapeDtypeStruct(sums.shape, jnp.float32),
        ),
        in_specs=[ANY] + [VMEM] * 5,
        out_specs=(VMEM, VMEM),
        input_output_aliases={4: 1},
        scratch_shapes=[
            pltpu.SMEM(pairs.shape, jnp.int32),
            pltpu.VMEM((2 * LANES, depth), jnp.bfloat16),
            pltpu.VMEM((depth, LANES), jnp.bfloat16),
            pltpu.VMEM((depth, LANES), jnp.bfloat16),
            pltpu.VMEM((GROUPS, extended, LANES), jnp.bfloat16),
            pltpu.VMEM((GROUPS, extended, LANES), jnp.bfloat16),
            pltpu.SemaphoreType.DMA,
        ],
        compiler_params=pltpu.CompilerParams(vmem_limit_bytes=(8 << 20) + devices * (5 << 17)),
        name="stack",
    )(pairs, *turned, sums, last)
    return stack


def on_device(samples, scales, bin_ids, owner_table):
    devices = lax.axis_size("chan")
    span = samples.shape[1] - 2 * LAG
    own = lax.axis_index("chan").reshape(1).astype(jnp.int32)

    def swap(value, offset):
        return lax.ppermute(value, "chan", [(i, i ^ offset) for i in range(devices)])

    piece = prep(samples, scales)
    pairs = find_pairs(devices, own, bin_ids, owner_table)
    members = devices // GROUPS
    own_column = jnp.zeros((members,) + piece.shape, piece.dtype).at[0].set(piece)
    plane = [swap(piece, 2)]
    for i in range(1, members):
        one = swap(piece, 4 * i)
        plane.append(swap(one, 2))
        own_column = own_column.at[i].set(one)
    side_column = swap(own_column, 1)
    own_plane = jnp.stack(plane)
    side_plane = swap(own_plane, 1)
    turned_0 = turn(own_column)
    turned_2, sums = early(devices, pairs, own_column, side_column)
    turned_1, sums = add_plane(devices, pairs, own_plane, sums)
    return stack_bin(
        devices, span, pairs, (turned_0, turned_1, turned_2), sums, side_plane
    )


def solution(mesh):
    placed = (P(("groups", "chan"), None), P(("groups", "chan")), P(), P())
    return jax.shard_map(
        on_device,
        mesh=mesh,
        in_specs=placed,
        out_specs=P(("groups", "chan"), None),
        check_vma=False,
    )
```

```python
import functools

import jax
import jax.numpy as jnp
from jax import lax
from jax.experimental import pallas as pl
from jax.experimental.pallas import tpu as pltpu
from jax.sharding import PartitionSpec as P

LAG = 32
LAGS = 65
CH = 16
STEP = 16
LANES = CH * STEP
FINE = 8
COARSE = 16
ROWS = FINE * COARSE
HEAD = ROWS + 8
REACH = LAG // STEP
SHIFTS = 2 * REACH + 1
OUT_LANES = LAGS * CH
BLEND = 32.0
HEADER = 8
GROUPS = 4

VMEM = pl.BlockSpec(memory_space=pltpu.VMEM)
SMEM = pl.BlockSpec(memory_space=pltpu.SMEM)
ANY = pl.BlockSpec(memory_space=pl.ANY)
HBM = pl.BlockSpec(memory_space=pltpu.HBM)


def piece_index(devices, offset):
    bits = (devices // GROUPS).bit_length() - 1
    return (offset >> 2) | (((offset >> 1) & 1) << bits) | ((offset & 1) << (bits + 1))


def prep_kernel(samples_ref, scales_ref, piece_ref, x_ref, s_ref, turned_ref, rows_ref, sem):
    copies = [
        pltpu.make_async_copy(samples_ref, x_ref, sem.at[0]),
        pltpu.make_async_copy(scales_ref, s_ref, sem.at[1]),
    ]
    for copy in copies:
        copy.start()
    copies[0].wait()
    samples = x_ref[...].astype(jnp.float32)
    granule = lax.broadcasted_iota(jnp.int32, (FINE, 128), 1) // CH
    for half in range(2):
        stripes = [
            samples[:, u2 * 128 : (u2 + 1) * 128] for u2 in range(8 * half, 8 * half + 8)
        ]
        turned_ref[half] = jnp.concatenate(stripes, axis=0).T
    for half in range(2):
        for part in range(2):
            tiles = [
                turned_ref[half, pl.ds(8 * part + k, FINE, stride=STEP), :] for k in range(8)
            ]
            for step in (1, 2, 4):
                upper = (granule & step) != 0
                for k in range(8):
                    if k & step:
                        continue
                    one, two = tiles[k], tiles[k + step]
                    tiles[k] = jnp.where(upper, pltpu.roll(two, CH * step, 1), one)
                    tiles[k + step] = jnp.where(upper, two, pltpu.roll(one, 128 - CH * step, 1))
            for k in range(8):
                rows_ref[part, pl.ds(8 * half + k, FINE, stride=COARSE), :] = tiles[k]
    for part in range(2):
        piece_ref[0:ROWS, part * 128 : (part + 1) * 128] = rows_ref[part].astype(jnp.bfloat16)
    copies[1].wait()
    scales = s_ref[...].astype(jnp.float32)
    piece_ref[ROWS:HEAD, :] = jnp.broadcast_to(
        jnp.concatenate([scales] * STEP, axis=1), (HEAD - ROWS, LANES)
    ).astype(jnp.bfloat16)


def prep(samples, scales):
    return pl.pallas_call(
        prep_kernel,
        out_shape=jax.ShapeDtypeStruct((HEAD, LANES), jnp.bfloat16),
        in_specs=[HBM, HBM],
        out_specs=VMEM,
        scratch_shapes=[
            pltpu.VMEM(samples.shape, jnp.bfloat16),
            pltpu.VMEM((1, CH), jnp.bfloat16),
            pltpu.VMEM((2, 128, 128), jnp.float32),
            pltpu.VMEM((2, ROWS, 128), jnp.float32),
            pltpu.SemaphoreType.DMA((2,)),
        ],
        compiler_params=pltpu.CompilerParams(vmem_limit_bytes=4 << 20),
        name="prep",
    )(
        pltpu.with_memory_space_constraint(samples, pltpu.HBM),
        pltpu.with_memory_space_constraint(scales.reshape(1, CH), pltpu.HBM),
    )


def pairs_kernel(devices, own_ref, bins_ref, owner_ref, list_ref):
    own = own_ref[0]
    members = devices // GROUPS
    own_bin = jnp.int32(0)
    for i in range(devices):
        own_bin = jnp.where(owner_ref[i] == own, i, own_bin)

    def row(p, found):
        found = list(found)
        cells = [bins_ref[p, q] for q in range(devices)]
        for q, cell in enumerate(cells):
            kind = q % GROUPS
            list_ref[HEADER + kind * devices * members + found[kind]] = p * members + q // GROUPS
            found[kind] = found[kind] + jnp.where(cell == own_bin, 1, 0)
        return tuple(found)

    found = lax.fori_loop(0, devices, row, (jnp.int32(0),) * GROUPS)
    list_ref[0] = own
    for kind in range(GROUPS):
        list_ref[1 + kind] = found[kind]


def find_pairs(devices, own, bin_ids, owner_table):
    return pl.pallas_call(
        functools.partial(pairs_kernel, devices),
        out_shape=jax.ShapeDtypeStruct((HEADER + devices * devices + 1,), jnp.int32),
        in_specs=[SMEM] * 3,
        out_specs=SMEM,
        compiler_params=pltpu.CompilerParams(vmem_limit_bytes=1 << 20),
        cost_estimate=pl.CostEstimate(flops=10_000_000, bytes_accessed=1 << 20, transcendentals=0),
        name="pairs",
    )(
        own,
        pltpu.with_memory_space_constraint(bin_ids, pltpu.HBM),
        pltpu.with_memory_space_constraint(owner_table, pltpu.HBM),
    )


def split_left(value):
    high = value.astype(jnp.bfloat16)
    wide = high.astype(jnp.float32)
    return high, (wide + BLEND * (value - wide)).astype(jnp.bfloat16)


def split_right(value):
    high = value.astype(jnp.bfloat16)
    wide = high.astype(jnp.float32)
    return high, (wide * (1.0 / BLEND) + (value - wide)).astype(jnp.bfloat16)


def inside_rows():
    row = lax.broadcasted_iota(jnp.int32, (ROWS, LANES), 0)
    u = FINE * (row % COARSE) + row // COARSE
    return (u >= REACH) & (u < ROWS - REACH)


def turn_group(load, members, turned_ref, high_ref, low_ref):
    inside = inside_rows()
    for i in range(members):
        scale = load(i, ROWS, ROWS + 1)
        high, low = split_left(jnp.where(inside, load(i, 0, ROWS) * scale, 0.0))
        for u1 in range(FINE):
            at = (u1 * members + i) * COARSE
            high_ref[at : at + COARSE, :] = high[u1 * COARSE : (u1 + 1) * COARSE]
            low_ref[at : at + COARSE, :] = low[u1 * COARSE : (u1 + 1) * COARSE]
    for k in range(0, members * ROWS, 128):
        turned_ref[0:LANES, k : k + 128] = high_ref[k : k + 128, :].T
        turned_ref[LANES : 2 * LANES, k : k + 128] = low_ref[k : k + 128, :].T


def loader(ref):
    return lambda i, start, stop: ref[i, start:stop, :].astype(jnp.float32)


def turn_kernel(x_ref, turned_ref, high_ref, low_ref):
    turn_group(loader(x_ref), x_ref.shape[0], turned_ref, high_ref, low_ref)


def turn(pieces):
    members = pieces.shape[0]
    return pl.pallas_call(
        turn_kernel,
        out_shape=jax.ShapeDtypeStruct((2 * LANES, members * ROWS), jnp.bfloat16),
        in_specs=[VMEM],
        out_specs=VMEM,
        scratch_shapes=[
            pltpu.VMEM((members * ROWS, LANES), jnp.bfloat16),
            pltpu.VMEM((members * ROWS, LANES), jnp.bfloat16),
        ],
        compiler_params=pltpu.CompilerParams(vmem_limit_bytes=(2 << 20) + members * (1 << 19)),
        cost_estimate=pl.CostEstimate(
            flops=members * 2_000_000, bytes_accessed=members << 18, transcendentals=0
        ),
        name="turn",
    )(pieces)


def add_pairs(devices, group, list_ref, x_ref, sums_ref):
    members = devices // GROUPS
    own = list_ref[0]
    kind = (own & 3) ^ (((group & 1) << 1) | (group >> 1))
    base = HEADER + kind * devices * members

    def add(place, carry):
        code = list_ref[base + place]
        i = piece_index(devices, own ^ (code >> (members.bit_length() - 1)))
        j = (code & (members - 1)) ^ (own >> 2)
        scale = x_ref[j, ROWS : ROWS + 1, :].astype(jnp.float32)
        sums_ref[i] = sums_ref[i] + x_ref[j, 0:ROWS, :].astype(jnp.float32) * scale
        return carry

    lax.fori_loop(0, list_ref[1 + kind], add, 0)


def early_kernel(
    devices, pairs_ref, column_ref, side_ref, turned_ref, sums_ref, list_ref, high_ref, low_ref, sem
):
    members = devices // GROUPS
    copy = pltpu.make_async_copy(pairs_ref, list_ref, sem)
    copy.start()
    sums_ref[...] = jnp.zeros_like(sums_ref)
    turn_group(loader(side_ref), members, turned_ref, high_ref, low_ref)
    copy.wait()
    for group, ref in ((0, column_ref), (2, side_ref)):
        add_pairs(devices, group, list_ref, ref, sums_ref)


def plane_kernel(
    devices, pairs_ref, plane_ref, _, turned_ref, sums_ref, list_ref, high_ref, low_ref, sem
):
    members = devices // GROUPS
    copy = pltpu.make_async_copy(pairs_ref, list_ref, sem)
    copy.start()
    turn_group(loader(plane_ref), members, turned_ref, high_ref, low_ref)
    copy.wait()
    add_pairs(devices, 1, list_ref, plane_ref, sums_ref)


def early(devices, pairs, column, side):
    members = devices // GROUPS
    return pl.pallas_call(
        functools.partial(early_kernel, devices),
        out_shape=(
            jax.ShapeDtypeStruct((2 * LANES, members * ROWS), jnp.bfloat16),
            jax.ShapeDtypeStruct((devices, ROWS, LANES), jnp.float32),
        ),
        in_specs=[ANY, VMEM, VMEM],
        out_specs=(VMEM, VMEM),
        scratch_shapes=[
            pltpu.SMEM(pairs.shape, jnp.int32),
            pltpu.VMEM((members * ROWS, LANES), jnp.bfloat16),
            pltpu.VMEM((members * ROWS, LANES), jnp.bfloat16),
            pltpu.SemaphoreType.DMA,
        ],
        compiler_params=pltpu.CompilerParams(vmem_limit_bytes=(2 << 20) + devices * (1 << 19)),
        cost_estimate=pl.CostEstimate(
            flops=devices * 2_000_000, bytes_accessed=devices << 18, transcendentals=0
        ),
        name="early",
    )(pairs, column, side)


def add_plane(devices, pairs, plane, sums):
    members = devices // GROUPS
    return pl.pallas_call(
        functools.partial(plane_kernel, devices),
        out_shape=(
            jax.ShapeDtypeStruct((2 * LANES, members * ROWS), jnp.bfloat16),
            jax.ShapeDtypeStruct(sums.shape, jnp.float32),
        ),
        in_specs=[ANY, VMEM, VMEM],
        out_specs=(VMEM, VMEM),
        input_output_aliases={2: 1},
        scratch_shapes=[
            pltpu.SMEM(pairs.shape, jnp.int32),
            pltpu.VMEM((members * ROWS, LANES), jnp.bfloat16),
            pltpu.VMEM((members * ROWS, LANES), jnp.bfloat16),
            pltpu.SemaphoreType.DMA,
        ],
        compiler_params=pltpu.CompilerParams(vmem_limit_bytes=(2 << 20) + devices * (1 << 19)),
        cost_estimate=pl.CostEstimate(
            flops=devices * 1_000_000, bytes_accessed=devices << 17, transcendentals=0
        ),
        name="plane",
    )(pairs, plane, sums)


def stack_kernel(
    devices, span, pairs_ref, a0_ref, a1_ref, a2_ref, _, x_ref, out_ref, sums_ref,
    list_ref, a3_ref, high_ref, low_ref, yh_ref, yl_ref, sem,
):
    members = devices // GROUPS
    depth = members * ROWS
    slab = members * COARSE
    copy = pltpu.make_async_copy(pairs_ref, list_ref, sem)
    copy.start()
    turn_group(loader(x_ref), members, a3_ref, high_ref, low_ref)
    copy.wait()
    add_pairs(devices, GROUPS - 1, list_ref, x_ref, sums_ref)

    def put(group, member, u1, value):
        high, low = split_right(value)
        at = ((u1 + REACH) * members + member) * COARSE
        yh_ref[group, at : at + COARSE, :] = high
        yl_ref[group, at : at + COARSE, :] = low

    products = [None] * SHIFTS
    for group, turned_ref in enumerate((a0_ref, a1_ref, a2_ref, a3_ref)):
        for member in range(members):
            total = sums_ref[group * members + member]
            parts = [total[u1 * COARSE : (u1 + 1) * COARSE] for u1 in range(FINE)]
            for u1 in range(FINE):
                put(group, member, u1, parts[u1])
            for u1 in range(REACH):
                put(group, member, u1 + FINE, pltpu.roll(parts[u1], COARSE - 1, 0))
            for u1 in range(FINE - REACH, FINE):
                put(group, member, u1 - FINE, pltpu.roll(parts[u1], 1, 0))
        for j in range(SHIFTS):
            rows = slice(j * slab, j * slab + depth)
            main = jnp.dot(
                turned_ref[0:LANES, :], yh_ref[group, rows, :], preferred_element_type=jnp.float32
            )
            rest = jnp.dot(
                turned_ref[LANES : 2 * LANES, :],
                yl_ref[group, rows, :],
                preferred_element_type=jnp.float32,
            )
            part = main * (1.0 - 1.0 / BLEND) + rest
            products[j] = part if group == 0 else products[j] + part
    product = jnp.concatenate(products, axis=1)
    stack = jnp.zeros((CH, OUT_LANES), jnp.float32)
    for v in range(STEP):
        stack = stack + product[CH * v : CH * (v + 1), CH * v : CH * v + OUT_LANES]
    count = sum(list_ref[1 + kind] for kind in range(GROUPS)).astype(jnp.float32)
    stack = stack / jnp.sqrt(jnp.full((CH, OUT_LANES), count * span, jnp.float32))
    for a in range(CH):
        out_ref[0:1, a * OUT_LANES : (a + 1) * OUT_LANES] = stack[a : a + 1]


def stack_bin(devices, span, pairs, turned, sums, last):
    members = devices // GROUPS
    depth = members * ROWS
    extended = members * COARSE * (FINE + 2 * REACH)
    stack, _ = pl.pallas_call(
        functools.partial(stack_kernel, devices, float(span)),
        out_shape=(
            jax.ShapeDtypeStruct((1, CH * OUT_LANES), jnp.float32),
            jax.ShapeDtypeStruct(sums.shape, jnp.float32),
        ),
        in_specs=[ANY] + [VMEM] * 5,
        out_specs=(VMEM, VMEM),
        input_output_aliases={4: 1},
        scratch_shapes=[
            pltpu.SMEM(pairs.shape, jnp.int32),
            pltpu.VMEM((2 * LANES, depth), jnp.bfloat16),
            pltpu.VMEM((depth, LANES), jnp.bfloat16),
            pltpu.VMEM((depth, LANES), jnp.bfloat16),
            pltpu.VMEM((GROUPS, extended, LANES), jnp.bfloat16),
            pltpu.VMEM((GROUPS, extended, LANES), jnp.bfloat16),
            pltpu.SemaphoreType.DMA,
        ],
        compiler_params=pltpu.CompilerParams(vmem_limit_bytes=(8 << 20) + devices * (5 << 17)),
        name="stack",
    )(pairs, *turned, sums, last)
    return stack


def on_device(samples, scales, bin_ids, owner_table):
    devices = lax.axis_size("chan")
    span = samples.shape[1] - 2 * LAG
    own = lax.axis_index("chan").reshape(1).astype(jnp.int32)

    def swap(value, offset):
        return lax.ppermute(value, "chan", [(i, i ^ offset) for i in range(devices)])

    piece = prep(samples, scales)
    pairs = find_pairs(devices, own, bin_ids, owner_table)
    members = devices // GROUPS
    own_column = jnp.zeros((members,) + piece.shape, piece.dtype).at[0].set(piece)
    plane = [swap(piece, 2)]
    for i in range(1, members):
        one = swap(piece, 4 * i)
        plane.append(swap(one, 2))
        own_column = own_column.at[i].set(one)
    side_column = swap(own_column, 1)
    first_rows = jnp.stack(plane[:-1])
    side_plane = jnp.concatenate([swap(first_rows, 1), swap(plane[-1], 1)[None]])
    own_plane = jnp.concatenate([first_rows, plane[-1][None]])
    turned_0 = turn(own_column)
    turned_2, sums = early(devices, pairs, own_column, side_column)
    turned_1, sums = add_plane(devices, pairs, own_plane, sums)
    return stack_bin(
        devices, span, pairs, (turned_0, turned_1, turned_2), sums, side_plane
    )


def solution(mesh):
    placed = (P(("groups", "chan"), None), P(("groups", "chan")), P(), P())
    return jax.shard_map(
        on_device,
        mesh=mesh,
        in_specs=placed,
        out_specs=P(("groups", "chan"), None),
        check_vma=False,
    )
```

```python
import functools

import jax
import jax.numpy as jnp
from jax import lax
from jax.experimental import pallas as pl
from jax.experimental.pallas import tpu as pltpu
from jax.sharding import PartitionSpec as P

LAG = 32
LAGS = 65
CH = 16
STEP = 16
LANES = CH * STEP
FINE = 8
COARSE = 16
ROWS = FINE * COARSE
HEAD = ROWS + 8
REACH = LAG // STEP
SHIFTS = 2 * REACH + 1
OUT_LANES = LAGS * CH
BLEND = 32.0
HEADER = 8
GROUPS = 4

VMEM = pl.BlockSpec(memory_space=pltpu.VMEM)
SMEM = pl.BlockSpec(memory_space=pltpu.SMEM)
ANY = pl.BlockSpec(memory_space=pl.ANY)
HBM = pl.BlockSpec(memory_space=pltpu.HBM)


def piece_index(devices, offset):
    bits = (devices // GROUPS).bit_length() - 1
    return (offset >> 2) | (((offset >> 1) & 1) << bits) | ((offset & 1) << (bits + 1))


def prep_kernel(samples_ref, scales_ref, piece_ref, x_ref, s_ref, turned_ref, rows_ref, sem):
    copies = [
        pltpu.make_async_copy(samples_ref, x_ref, sem.at[0]),
        pltpu.make_async_copy(scales_ref, s_ref, sem.at[1]),
    ]
    for copy in copies:
        copy.start()
    copies[0].wait()
    samples = x_ref[...].astype(jnp.float32)
    granule = lax.broadcasted_iota(jnp.int32, (FINE, 128), 1) // CH
    for half in range(2):
        stripes = [
            samples[:, u2 * 128 : (u2 + 1) * 128] for u2 in range(8 * half, 8 * half + 8)
        ]
        turned_ref[half] = jnp.concatenate(stripes, axis=0).T
    for half in range(2):
        for part in range(2):
            tiles = [
                turned_ref[half, pl.ds(8 * part + k, FINE, stride=STEP), :] for k in range(8)
            ]
            for step in (1, 2, 4):
                upper = (granule & step) != 0
                for k in range(8):
                    if k & step:
                        continue
                    one, two = tiles[k], tiles[k + step]
                    tiles[k] = jnp.where(upper, pltpu.roll(two, CH * step, 1), one)
                    tiles[k + step] = jnp.where(upper, two, pltpu.roll(one, 128 - CH * step, 1))
            for k in range(8):
                rows_ref[part, pl.ds(8 * half + k, FINE, stride=COARSE), :] = tiles[k]
    for part in range(2):
        piece_ref[0:ROWS, part * 128 : (part + 1) * 128] = rows_ref[part].astype(jnp.bfloat16)
    copies[1].wait()
    scales = s_ref[...].astype(jnp.float32)
    piece_ref[ROWS:HEAD, :] = jnp.broadcast_to(
        jnp.concatenate([scales] * STEP, axis=1), (HEAD - ROWS, LANES)
    ).astype(jnp.bfloat16)


def prep(samples, scales):
    return pl.pallas_call(
        prep_kernel,
        out_shape=jax.ShapeDtypeStruct((HEAD, LANES), jnp.bfloat16),
        in_specs=[HBM, HBM],
        out_specs=VMEM,
        scratch_shapes=[
            pltpu.VMEM(samples.shape, jnp.bfloat16),
            pltpu.VMEM((1, CH), jnp.bfloat16),
            pltpu.VMEM((2, 128, 128), jnp.float32),
            pltpu.VMEM((2, ROWS, 128), jnp.float32),
            pltpu.SemaphoreType.DMA((2,)),
        ],
        compiler_params=pltpu.CompilerParams(vmem_limit_bytes=4 << 20),
        name="prep",
    )(
        pltpu.with_memory_space_constraint(samples, pltpu.HBM),
        pltpu.with_memory_space_constraint(scales.reshape(1, CH), pltpu.HBM),
    )


def pairs_kernel(devices, own_ref, bins_ref, owner_ref, list_ref):
    own = own_ref[0]
    members = devices // GROUPS
    own_bin = jnp.int32(0)
    for i in range(devices):
        own_bin = jnp.where(owner_ref[i] == own, i, own_bin)

    def row(p, found):
        found = list(found)
        cells = [bins_ref[p, q] for q in range(devices)]
        for q, cell in enumerate(cells):
            kind = q % GROUPS
            list_ref[HEADER + kind * devices * members + found[kind]] = p * members + q // GROUPS
            found[kind] = found[kind] + jnp.where(cell == own_bin, 1, 0)
        return tuple(found)

    found = lax.fori_loop(0, devices, row, (jnp.int32(0),) * GROUPS)
    list_ref[0] = own
    for kind in range(GROUPS):
        list_ref[1 + kind] = found[kind]


def find_pairs(devices, own, bin_ids, owner_table):
    return pl.pallas_call(
        functools.partial(pairs_kernel, devices),
        out_shape=jax.ShapeDtypeStruct((HEADER + devices * devices + 1,), jnp.int32),
        in_specs=[SMEM] * 3,
        out_specs=SMEM,
        compiler_params=pltpu.CompilerParams(vmem_limit_bytes=1 << 20),
        cost_estimate=pl.CostEstimate(flops=10_000_000, bytes_accessed=1 << 20, transcendentals=0),
        name="pairs",
    )(
        own,
        pltpu.with_memory_space_constraint(bin_ids, pltpu.HBM),
        pltpu.with_memory_space_constraint(owner_table, pltpu.HBM),
    )


def split_left(value):
    high = value.astype(jnp.bfloat16)
    wide = high.astype(jnp.float32)
    return high, (wide + BLEND * (value - wide)).astype(jnp.bfloat16)


def split_right(value):
    high = value.astype(jnp.bfloat16)
    wide = high.astype(jnp.float32)
    return high, (wide * (1.0 / BLEND) + (value - wide)).astype(jnp.bfloat16)


def inside_rows():
    row = lax.broadcasted_iota(jnp.int32, (ROWS, LANES), 0)
    u = FINE * (row % COARSE) + row // COARSE
    return (u >= REACH) & (u < ROWS - REACH)


def turn_group(load, members, turned_ref, high_ref, low_ref):
    inside = inside_rows()
    for i in range(members):
        scale = load(i, ROWS, ROWS + 1)
        high, low = split_left(jnp.where(inside, load(i, 0, ROWS) * scale, 0.0))
        for u1 in range(FINE):
            at = (u1 * members + i) * COARSE
            high_ref[at : at + COARSE, :] = high[u1 * COARSE : (u1 + 1) * COARSE]
            low_ref[at : at + COARSE, :] = low[u1 * COARSE : (u1 + 1) * COARSE]
    for k in range(0, members * ROWS, 128):
        turned_ref[0:LANES, k : k + 128] = high_ref[k : k + 128, :].T
        turned_ref[LANES : 2 * LANES, k : k + 128] = low_ref[k : k + 128, :].T


def loader(ref):
    return lambda i, start, stop: ref[i, start:stop, :].astype(jnp.float32)


def turn_kernel(x_ref, turned_ref, high_ref, low_ref):
    turn_group(loader(x_ref), x_ref.shape[0], turned_ref, high_ref, low_ref)


def turn(pieces):
    members = pieces.shape[0]
    return pl.pallas_call(
        turn_kernel,
        out_shape=jax.ShapeDtypeStruct((2 * LANES, members * ROWS), jnp.bfloat16),
        in_specs=[VMEM],
        out_specs=VMEM,
        scratch_shapes=[
            pltpu.VMEM((members * ROWS, LANES), jnp.bfloat16),
            pltpu.VMEM((members * ROWS, LANES), jnp.bfloat16),
        ],
        compiler_params=pltpu.CompilerParams(vmem_limit_bytes=(2 << 20) + members * (1 << 19)),
        cost_estimate=pl.CostEstimate(
            flops=members * 2_000_000, bytes_accessed=members << 18, transcendentals=0
        ),
        name="turn",
    )(pieces)


def add_pairs(devices, group, list_ref, x_ref, sums_ref):
    members = devices // GROUPS
    own = list_ref[0]
    kind = (own & 3) ^ (((group & 1) << 1) | (group >> 1))
    base = HEADER + kind * devices * members

    def add(place, carry):
        code = list_ref[base + place]
        i = piece_index(devices, own ^ (code >> (members.bit_length() - 1)))
        j = (code & (members - 1)) ^ (own >> 2)
        scale = x_ref[j, ROWS : ROWS + 1, :].astype(jnp.float32)
        sums_ref[i] = sums_ref[i] + x_ref[j, 0:ROWS, :].astype(jnp.float32) * scale
        return carry

    lax.fori_loop(0, list_ref[1 + kind], add, 0)


def early_kernel(
    devices, pairs_ref, column_ref, side_ref, turned_ref, sums_ref, list_ref, high_ref, low_ref, sem
):
    members = devices // GROUPS
    copy = pltpu.make_async_copy(pairs_ref, list_ref, sem)
    copy.start()
    sums_ref[...] = jnp.zeros_like(sums_ref)
    turn_group(loader(side_ref), members, turned_ref, high_ref, low_ref)
    copy.wait()
    for group, ref in ((0, column_ref), (2, side_ref)):
        add_pairs(devices, group, list_ref, ref, sums_ref)


def plane_kernel(
    devices, pairs_ref, plane_ref, _, turned_ref, sums_ref, list_ref, high_ref, low_ref, sem
):
    members = devices // GROUPS
    copy = pltpu.make_async_copy(pairs_ref, list_ref, sem)
    copy.start()
    turn_group(loader(plane_ref), members, turned_ref, high_ref, low_ref)
    copy.wait()
    add_pairs(devices, 1, list_ref, plane_ref, sums_ref)


def early(devices, pairs, column, side):
    members = devices // GROUPS
    return pl.pallas_call(
        functools.partial(early_kernel, devices),
        out_shape=(
            jax.ShapeDtypeStruct((2 * LANES, members * ROWS), jnp.bfloat16),
            jax.ShapeDtypeStruct((devices, ROWS, LANES), jnp.float32),
        ),
        in_specs=[ANY, VMEM, VMEM],
        out_specs=(VMEM, VMEM),
        scratch_shapes=[
            pltpu.SMEM(pairs.shape, jnp.int32),
            pltpu.VMEM((members * ROWS, LANES), jnp.bfloat16),
            pltpu.VMEM((members * ROWS, LANES), jnp.bfloat16),
            pltpu.SemaphoreType.DMA,
        ],
        compiler_params=pltpu.CompilerParams(vmem_limit_bytes=(2 << 20) + devices * (1 << 19)),
        cost_estimate=pl.CostEstimate(
            flops=devices * 2_000_000, bytes_accessed=devices << 18, transcendentals=0
        ),
        name="early",
    )(pairs, column, side)


def add_plane(devices, pairs, plane, sums):
    members = devices // GROUPS
    return pl.pallas_call(
        functools.partial(plane_kernel, devices),
        out_shape=(
            jax.ShapeDtypeStruct((2 * LANES, members * ROWS), jnp.bfloat16),
            jax.ShapeDtypeStruct(sums.shape, jnp.float32),
        ),
        in_specs=[ANY, VMEM, VMEM],
        out_specs=(VMEM, VMEM),
        input_output_aliases={2: 1},
        scratch_shapes=[
            pltpu.SMEM(pairs.shape, jnp.int32),
            pltpu.VMEM((members * ROWS, LANES), jnp.bfloat16),
            pltpu.VMEM((members * ROWS, LANES), jnp.bfloat16),
            pltpu.SemaphoreType.DMA,
        ],
        compiler_params=pltpu.CompilerParams(vmem_limit_bytes=(2 << 20) + devices * (1 << 19)),
        cost_estimate=pl.CostEstimate(
            flops=devices * 1_000_000, bytes_accessed=devices << 17, transcendentals=0
        ),
        name="plane",
    )(pairs, plane, sums)


def stack_kernel(
    devices, span, pairs_ref, a0_ref, a1_ref, a2_ref, _, x_ref, out_ref, sums_ref,
    list_ref, a3_ref, high_ref, low_ref, yh_ref, yl_ref, sem,
):
    members = devices // GROUPS
    depth = members * ROWS
    slab = members * COARSE
    copy = pltpu.make_async_copy(pairs_ref, list_ref, sem)
    copy.start()
    turn_group(loader(x_ref), members, a3_ref, high_ref, low_ref)
    copy.wait()
    add_pairs(devices, GROUPS - 1, list_ref, x_ref, sums_ref)

    def put(group, member, u1, value):
        high, low = split_right(value)
        at = ((u1 + REACH) * members + member) * COARSE
        yh_ref[group, at : at + COARSE, :] = high
        yl_ref[group, at : at + COARSE, :] = low

    products = [None] * SHIFTS
    for group, turned_ref in enumerate((a0_ref, a1_ref, a2_ref, a3_ref)):
        for member in range(members):
            total = sums_ref[group * members + member]
            parts = [total[u1 * COARSE : (u1 + 1) * COARSE] for u1 in range(FINE)]
            for u1 in range(FINE):
                put(group, member, u1, parts[u1])
            for u1 in range(REACH):
                put(group, member, u1 + FINE, pltpu.roll(parts[u1], COARSE - 1, 0))
            for u1 in range(FINE - REACH, FINE):
                put(group, member, u1 - FINE, pltpu.roll(parts[u1], 1, 0))
        for j in range(SHIFTS):
            rows = slice(j * slab, j * slab + depth)
            main = jnp.dot(
                turned_ref[0:LANES, :], yh_ref[group, rows, :], preferred_element_type=jnp.float32
            )
            rest = jnp.dot(
                turned_ref[LANES : 2 * LANES, :],
                yl_ref[group, rows, :],
                preferred_element_type=jnp.float32,
            )
            part = main * (1.0 - 1.0 / BLEND) + rest
            products[j] = part if group == 0 else products[j] + part
    product = jnp.concatenate(products, axis=1)
    stack = jnp.zeros((CH, OUT_LANES), jnp.float32)
    for v in range(STEP):
        stack = stack + product[CH * v : CH * (v + 1), CH * v : CH * v + OUT_LANES]
    count = sum(list_ref[1 + kind] for kind in range(GROUPS)).astype(jnp.float32)
    stack = stack / jnp.sqrt(jnp.full((CH, OUT_LANES), count * span, jnp.float32))
    for a in range(CH):
        out_ref[0:1, a * OUT_LANES : (a + 1) * OUT_LANES] = stack[a : a + 1]


def stack_bin(devices, span, pairs, turned, sums, last):
    members = devices // GROUPS
    depth = members * ROWS
    extended = members * COARSE * (FINE + 2 * REACH)
    stack, _ = pl.pallas_call(
        functools.partial(stack_kernel, devices, float(span)),
        out_shape=(
            jax.ShapeDtypeStruct((1, CH * OUT_LANES), jnp.float32),
            jax.ShapeDtypeStruct(sums.shape, jnp.float32),
        ),
        in_specs=[ANY] + [VMEM] * 5,
        out_specs=(VMEM, VMEM),
        input_output_aliases={4: 1},
        scratch_shapes=[
            pltpu.SMEM(pairs.shape, jnp.int32),
            pltpu.VMEM((2 * LANES, depth), jnp.bfloat16),
            pltpu.VMEM((depth, LANES), jnp.bfloat16),
            pltpu.VMEM((depth, LANES), jnp.bfloat16),
            pltpu.VMEM((GROUPS, extended, LANES), jnp.bfloat16),
            pltpu.VMEM((GROUPS, extended, LANES), jnp.bfloat16),
            pltpu.SemaphoreType.DMA,
        ],
        compiler_params=pltpu.CompilerParams(vmem_limit_bytes=(8 << 20) + devices * (5 << 17)),
        name="stack",
    )(pairs, *turned, sums, last)
    return stack


def on_device(samples, scales, bin_ids, owner_table):
    devices = lax.axis_size("chan")
    span = samples.shape[1] - 2 * LAG
    own = lax.axis_index("chan").reshape(1).astype(jnp.int32)

    def swap(value, offset):
        return lax.ppermute(value, "chan", [(i, i ^ offset) for i in range(devices)])

    piece = prep(samples, scales)
    pairs = find_pairs(devices, own, bin_ids, owner_table)
    members = devices // GROUPS
    own_column = jnp.zeros((members,) + piece.shape, piece.dtype).at[0].set(piece)
    plane = [swap(piece, 2)]
    for i in range(1, members):
        cross = int(i == members - 1)
        one = swap(piece, 4 * i + cross)
        plane.append(swap(one, 2 + cross))
        own_column = own_column.at[i].set(one)
    side_column = swap(own_column, 1)
    crossed = own_column[members - 1]
    own_column = own_column.at[members - 1].set(side_column[members - 1])
    side_column = side_column.at[members - 1].set(crossed)
    first_rows = jnp.stack(plane[:-1])
    side_plane = jnp.concatenate([swap(first_rows, 1), swap(plane[-1], 1)[None]])
    own_plane = jnp.concatenate([first_rows, plane[-1][None]])
    turned_0 = turn(own_column)
    turned_2, sums = early(devices, pairs, own_column, side_column)
    turned_1, sums = add_plane(devices, pairs, own_plane, sums)
    return stack_bin(
        devices, span, pairs, (turned_0, turned_1, turned_2), sums, side_plane
    )


def solution(mesh):
    placed = (P(("groups", "chan"), None), P(("groups", "chan")), P(), P())
    return jax.shard_map(
        on_device,
        mesh=mesh,
        in_specs=placed,
        out_specs=P(("groups", "chan"), None),
        check_vma=False,
    )
```
